128 devices in a mesh: fsdp: 4 (over y), ctx: 32 (over z, x, core).
Axes of the slice: x: 4, y: 4, z: 4, core: 2. Of those that a mesh axis runs over, the one named last changes fastest.
Arguments:
- tokens: bfloat16 [12, 4096, 2560], P('fsdp', 'ctx'), may hold values from -6 to 6
- doc_ids: int32 [12, 4096], P('fsdp', 'ctx'), may hold values from 0 to 15, never falling along the last dimension, each value on 1 to 2048 neighbouring positions
- cotangent: bfloat16 [12, 4096, 2560], P('fsdp', 'ctx'), may hold values from -6 to 6
- input_gain: float32 [2560], replicated, may hold values from 0.5 to 1.5
- query_weight: bfloat16 [2560, 1024], P('fsdp'), may hold values from -1 to 1
- key_weight: bfloat16 [2560, 512], P('fsdp'), may hold values from -1 to 1
- value_weight: bfloat16 [2560, 512], P('fsdp'), may hold values from -0.125 to 0.125
- output_weight: bfloat16 [1024, 2560], P('fsdp'), may hold values from -0.1875 to 0.1875
- query_gain: float32 [256], replicated, may hold values from 0 to 8
- key_gain: float32 [256], replicated, may hold values from 0 to 8
- post_gain: float32 [2560], replicated, may hold values from 0.25 to 1.75
Outputs:
- layer_out: bfloat16 [12, 4096, 2560], P('fsdp', 'ctx')
- tokens_grad: bfloat16 [12, 4096, 2560], P('fsdp', 'ctx')
- query_grad: float32 [2560, 1024], P('ctx', 'fsdp')
- key_grad: float32 [2560, 512], P('ctx', 'fsdp')
- value_grad: float32 [2560, 512], P('ctx', 'fsdp')
- output_grad: float32 [1024, 2560], P('ctx', 'fsdp')
The draws below stay inside these ranges and needn't reach their ends.
Inputs may be any that keep to these rules, and one draw needn't show every extreme that they name: `doc_ids`: along each sequence the document number never falls from one position to the next.
All inputs are finite; a program needn't handle non-finite values.
Results may differ from the reference program's by a relative error of at most 0.024.
The reference program's roundings to bfloat16 on the way (of `normed`, `values`, `soft_weights`, `attended`, `grad_projected`, `grad_attended` and `grad_scores`) count: a program that leaves them out, or rounds other values in their place, can miss the bound.
Values may be sent and summed in bfloat16 or wider, within the bound.
A program may use at most 192 MiB of HBM per device.

```python
import math
import jax
import jax.numpy as jnp
import numpy as np
from jax import lax

D = 2560
DH = 256
WINDOW = 1024
HQ = 4
HK = 2
SHARD = 128
SEQ_DEV = 3
DOCS = 16
SEQS = 12
LENGTH = 4096
N_FSDP = 4
N_CTX = 32


def query_base(key):
    raw = jax.random.normal(jax.random.fold_in(key, 101), (D, HQ * DH), jnp.float32)
    return jnp.clip(raw, -6.0, 6.0) * D ** (-0.5)


def draw_query_weight(key, part):
    return query_base(key).astype(jnp.bfloat16)


def draw_key_weight(key, part):
    noise = jax.random.normal(jax.random.fold_in(key, 102), (D, HK * DH), jnp.float32)
    noise = jnp.clip(noise, -6.0, 6.0) * D ** (-0.5)
    return noise.astype(jnp.bfloat16)


def gain_values(key, salt, top):
    spread = jax.random.uniform(jax.random.fold_in(key, salt), (DH,), jnp.float32)
    return 0.5 * jnp.exp(spread * jnp.log(top / 0.5))


def draw_query_gain(key, part):
    return gain_values(key, 201, 2.0)


def draw_key_gain(key, part):
    return gain_values(key, 202, 2.0)


def level_of(rng, shape, split, least, top_value):
    loudness = 1.0
    for axis_at, blocks in split:
        draws = jax.random.uniform(jax.random.fold_in(jax.random.fold_in(rng, 6), axis_at), (blocks,), jnp.float32, least / len(split), top_value / len(split))
        loudness = loudness * jnp.repeat(jnp.exp(draws), shape[axis_at] // blocks).reshape((-1,) + (1,) * (len(shape) - 1 - axis_at))
    return loudness


def profile(number_of, total, bound, skew):
    weights = [(1 << 20) // math.isqrt(grade ** skew) + 1 for grade in range(2, number_of + 1)]
    surplus, given = total - bound - (number_of - 1), [1] * (number_of - 1)
    while surplus > 0:
        candidates = [i for i in range(number_of - 1) if given[i] < bound]
        pool, budget = sum([weights[i] for i in candidates]), surplus
        for i in candidates:
            addition = min(bound - given[i], max(1, budget * weights[i] // pool), surplus)
            given[i] = given[i] + addition
            surplus = surplus - addition
    return np.array([bound] + given)


def uneven(rng, count, total, reach, slope):
    if count == 2:
        one = jax.random.randint(rng, (), max(1, total - reach), min(reach, total - 1) + 1)
        return jnp.stack([one, total - one])
    lengths = jnp.asarray(profile(count, total, reach, slope), jnp.int32)
    couples = (count - 1) // 2
    source_of, sink = lengths[1:1 + 2 * couples:2], lengths[2:2 + 2 * couples:2]
    margin = jnp.minimum(source_of - 1, reach - sink)
    passed = jax.random.randint(jax.random.fold_in(rng, 1), (couples,), 0, 1 << 20) % (margin + 1)
    lengths = lengths.at[1:1 + 2 * couples:2].set(source_of - passed).at[2:2 + 2 * couples:2].set(sink + passed)
    return lengths[jax.random.permutation(jax.random.fold_in(rng, 2), count)]


def gaussian(own_key, extent, deviation, most, pieces=(), held_as=jnp.bfloat16):
    entries = jax.random.normal(own_key, extent, jnp.float32) * deviation
    if len(pieces) > 0:
        entries = level_of(own_key, extent, pieces, -0.22, 0.18) * entries
    return jnp.clip(entries, min=-most, max=most).astype(held_as)


def setup_inputs(seed: int = 0) -> dict:
    streams_of = jax.random.split(jax.random.key(seed), 12)
    return {
        "tokens": gaussian(streams_of[0], (SEQS, LENGTH, D), 1.0, 6.0, ((0, 4), (1, 32))),
        "doc_ids": jax.vmap(lambda own: jnp.searchsorted(jnp.cumsum(uneven(own, DOCS, LENGTH, LENGTH // 2, 2)), jnp.arange(LENGTH), side="right"))(jax.random.split(streams_of[1], SEQS)).reshape((SEQS, LENGTH)).astype(jnp.int32),
        "cotangent": gaussian(streams_of[2], (SEQS, LENGTH, D), 1.0, 6.0, ((0, 4), (1, 32))),
        "input_gain": jnp.clip(1.0 + 0.1 * jax.random.normal(streams_of[3], (D,), jnp.float32), 0.5, 1.5),
        "query_weight": draw_query_weight(jax.random.fold_in(streams_of[11], 71), 0),
        "key_weight": draw_key_weight(jax.random.fold_in(streams_of[11], 71), 0),
        "value_weight": gaussian(streams_of[6], (D, HK * DH), D ** -0.5, 0.125, ((0, 4),)),
        "output_weight": gaussian(streams_of[7], (HQ * DH, D), (HQ * DH) ** -0.5, 0.1875, ((0, 4),)),
        "query_gain": draw_query_gain(jax.random.fold_in(streams_of[11], 71), 0),
        "key_gain": draw_key_gain(jax.random.fold_in(streams_of[11], 71), 0),
        "post_gain": jnp.clip(1.0 + 0.15 * jax.random.normal(streams_of[10], (D,), jnp.float32), 0.25, 1.75),
    }


epsilon = 1e-06
rope_base = 10000.0
query_factor = 0.0625

def rounded(values):
    return lax.optimization_barrier(values.astype(jnp.bfloat16))

def norm_scale(values, gain):
    mean_square = lax.optimization_barrier(jnp.mean(values * values, axis=-1, keepdims=True))
    return values * lax.rsqrt(mean_square + epsilon) * gain

def rotate(values, positions):
    half_width = values.shape[-1] // 2
    exponents = jnp.arange(half_width, dtype=jnp.int32).astype(jnp.float32) * (2.0 / values.shape[-1])
    angles = positions.astype(jnp.float32)[..., None] * rope_base ** (-exponents)
    cosine = jnp.cos(angles)[..., None, :]
    sine = jnp.sin(angles)[..., None, :]
    first_half = values[..., :half_width]
    second_half = values[..., half_width:]
    return jnp.concatenate([first_half * cosine - second_half * sine, second_half * cosine + first_half * sine], axis=-1)

def head_norm(raw, gain, positions, factor):
    shaped = raw.reshape(raw.shape[:-1] + (raw.shape[-1] // gain.shape[0], gain.shape[0]))
    return (rotate(norm_scale(shaped, gain), positions) * factor).reshape(raw.shape)

def split_heads(queries, keys, values):
    batch, rows, _ = queries.shape
    columns = keys.shape[1]
    kv_heads = keys.shape[-1] // DH
    ratio = queries.shape[-1] // keys.shape[-1]
    query_heads = queries.astype(jnp.float32).reshape(batch, rows, kv_heads, ratio, DH)
    key_heads = keys.astype(jnp.float32).reshape(batch, columns, kv_heads, DH)
    value_heads = values.astype(jnp.float32).reshape(batch, columns, kv_heads, DH)
    return (query_heads, key_heads, value_heads)

def attend(queries, keys, values, allowed):
    batch, rows, _ = queries.shape
    query_heads, key_heads, value_heads = split_heads(queries, keys, values)
    scores = jnp.einsum('bsgrd,bkgd->bgrsk', query_heads, key_heads)
    mask = allowed[:, None, None]
    masked = jnp.where(mask, scores, -1e+30)
    highest = lax.optimization_barrier(jnp.max(masked, axis=-1, keepdims=True))
    raised = jnp.where(mask, jnp.exp(masked - highest), 0.0)
    probabilities = raised / lax.optimization_barrier(jnp.sum(raised, axis=-1, keepdims=True))
    soft_weights = rounded(probabilities)
    attended = jnp.einsum('bgrsk,bkgd->bsgrd', soft_weights.astype(jnp.float32), value_heads)
    return (rounded(attended.reshape(batch, rows, -1)), probabilities, soft_weights)

def attend_back(queries, keys, values, probabilities, soft_weights, grad_attended):
    batch, rows, _ = queries.shape
    columns = keys.shape[1]
    query_heads, key_heads, value_heads = split_heads(queries, keys, values)
    grad_heads = grad_attended.astype(jnp.float32).reshape(query_heads.shape)
    grad_values = jnp.einsum('bgrsk,bsgrd->bkgd', soft_weights.astype(jnp.float32), grad_heads)
    grad_weights = jnp.einsum('bsgrd,bkgd->bgrsk', grad_heads, value_heads)
    grad_scores = probabilities * (grad_weights - lax.optimization_barrier(jnp.sum(probabilities * grad_weights, axis=-1, keepdims=True)))
    score_grads = rounded(grad_scores).astype(jnp.float32)
    grad_queries = jnp.einsum('bgrsk,bkgd->bsgrd', score_grads, key_heads)
    grad_keys = jnp.einsum('bgrsk,bsgrd->bkgd', score_grads, query_heads)
    return (grad_queries.reshape(batch, rows, -1), grad_keys.reshape(batch, columns, -1), grad_values.reshape(batch, columns, -1))

def reference(tokens, doc_ids, cotangent, input_gain, query_weight, key_weight, value_weight, output_weight, query_gain, key_gain, post_gain):
    reach_blocks = WINDOW // SHARD
    block_count = N_CTX
    span_keys = (reach_blocks + 1) * SHARD
    kv_width = HK * DH
    heads_width = HQ * DH
    outs_forward = []
    outs_grad = []
    sums = (jnp.zeros((D, heads_width), jnp.float32), jnp.zeros((D, kv_width), jnp.float32), jnp.zeros((D, kv_width), jnp.float32), jnp.zeros((heads_width, D), jnp.float32))

    def windows(array):
        blocks = array.reshape((SEQ_DEV, block_count, SHARD) + array.shape[2:])
        widths = [(0, 0), (reach_blocks, 0)] + [(0, 0)] * (blocks.ndim - 2)
        padded = jnp.pad(blocks, widths, constant_values=-1 if array.dtype == jnp.int32 else 0)
        slots = jnp.stack([padded[:, slot:slot + block_count] for slot in range(reach_blocks + 1)], axis=2)
        return slots.reshape((SEQ_DEV * block_count, span_keys) + array.shape[2:])

    def tiles(array):
        shaped = array.reshape(SEQ_DEV, block_count, SHARD, array.shape[-1])
        return shaped.transpose(1, 0, 2, 3).reshape(block_count, SEQ_DEV * SHARD, array.shape[-1])

    def accumulate(carry, items):
        normed_tile, query_tile, key_tile, value_tile, attended_tile, projected_tile = items
        terms = (jnp.dot(normed_tile.T, query_tile, preferred_element_type=jnp.float32), jnp.dot(normed_tile.T, key_tile, preferred_element_type=jnp.float32), jnp.dot(normed_tile.T, value_tile, preferred_element_type=jnp.float32), jnp.dot(attended_tile.T, projected_tile, preferred_element_type=jnp.float32))
        return (tuple((total + rounded(term).astype(jnp.float32) for total, term in zip(carry, terms))), None)
    for group in range(N_FSDP):
        lower = group * SEQ_DEV
        tokens_wide = tokens[lower:lower + SEQ_DEV].astype(jnp.float32)
        group_docs = doc_ids[lower:lower + SEQ_DEV]
        upstream = cotangent[lower:lower + SEQ_DEV].astype(jnp.float32)
        normed = rounded(norm_scale(tokens_wide, input_gain))
        flat_rows = normed.reshape(-1, D)
        query_raw = jnp.dot(flat_rows, query_weight, preferred_element_type=jnp.float32).reshape(SEQ_DEV, LENGTH, -1)
        key_raw = jnp.dot(flat_rows, key_weight, preferred_element_type=jnp.float32).reshape(SEQ_DEV, LENGTH, -1)
        values = rounded(jnp.dot(flat_rows, value_weight, preferred_element_type=jnp.float32)).reshape(SEQ_DEV, LENGTH, -1)
        positions = jnp.broadcast_to(jnp.arange(LENGTH, dtype=jnp.int32)[None], (SEQ_DEV, LENGTH))

        def prepare_query(raw):
            return head_norm(raw, query_gain, positions, query_factor)

        def prepare_key(raw):
            return head_norm(raw, key_gain, positions, 1.0)
        queries = rounded(prepare_query(query_raw))
        keys = rounded(prepare_key(key_raw))
        key_window = windows(keys)
        value_window = windows(values)
        key_docs = windows(group_docs)
        block_starts = (jnp.arange(block_count, dtype=jnp.int32)[:, None] - reach_blocks) * SHARD
        key_positions = block_starts + jnp.arange(span_keys, dtype=jnp.int32)[None]
        key_positions = jnp.broadcast_to(key_positions[None], (SEQ_DEV, block_count, span_keys)).reshape(-1, span_keys)
        query_positions = positions.reshape(-1, SHARD)
        query_docs = group_docs.reshape(-1, SHARD)
        allowed = (key_docs[:, None, :] == query_docs[:, :, None]) & (key_positions[:, None, :] >= 0) & (key_positions[:, None, :] <= query_positions[:, :, None]) & (key_positions[:, None, :] > query_positions[:, :, None] - WINDOW)
        query_blocks = queries.reshape(-1, SHARD, heads_width)
        attended, probabilities, soft_weights = attend(query_blocks, key_window, value_window, allowed)
        attended_rows = attended.reshape(-1, heads_width)
        projected = jnp.dot(attended_rows, output_weight, preferred_element_type=jnp.float32).reshape(SEQ_DEV, LENGTH, D)
        outs_forward.append((tokens_wide + norm_scale(projected, post_gain)).astype(jnp.bfloat16))
        _, post_back = jax.vjp(lambda inner: norm_scale(inner, post_gain), projected)
        grad_projected = rounded(post_back(upstream)[0]).reshape(-1, D)
        grad_attended = rounded(jnp.dot(grad_projected, output_weight.T, preferred_element_type=jnp.float32))
        grad_attended = grad_attended.reshape(-1, SHARD, heads_width)
        grad_queries, grad_keys, grad_values = attend_back(query_blocks, key_window, value_window, probabilities, soft_weights, grad_attended)
        grad_pairs = jnp.stack([grad_keys, grad_values]).reshape(2, SEQ_DEV, block_count, reach_blocks + 1, SHARD, kv_width)
        pair_total = grad_pairs[:, :, :, reach_blocks]
        for distance in range(1, reach_blocks + 1):
            if distance < block_count:
                piece = rounded(grad_pairs[:, :, distance:, reach_blocks - distance]).astype(jnp.float32)
                pair_total = pair_total + jnp.pad(piece, ((0, 0), (0, 0), (0, distance), (0, 0), (0, 0)))
        key_total = pair_total[0].reshape(SEQ_DEV, LENGTH, kv_width)
        value_total = pair_total[1].reshape(SEQ_DEV, LENGTH, kv_width)
        _, query_back = jax.vjp(prepare_query, query_raw)
        _, key_back = jax.vjp(prepare_key, key_raw)
        query_delta = rounded(query_back(grad_queries.reshape(SEQ_DEV, LENGTH, heads_width))[0]).reshape(-1, heads_width)
        key_delta = rounded(key_back(key_total)[0]).reshape(-1, kv_width)
        value_delta = rounded(value_total).reshape(-1, kv_width)
        grad_normed = jnp.dot(query_delta, query_weight.T, preferred_element_type=jnp.float32) + jnp.dot(key_delta, key_weight.T, preferred_element_type=jnp.float32) + jnp.dot(value_delta, value_weight.T, preferred_element_type=jnp.float32)
        _, input_back = jax.vjp(lambda inner: norm_scale(inner, input_gain), tokens_wide)
        outs_grad.append((upstream + input_back(grad_normed.reshape(SEQ_DEV, LENGTH, D))[0]).astype(jnp.bfloat16))
        sums, _ = lax.scan(accumulate, sums, (tiles(flat_rows), tiles(query_delta), tiles(key_delta), tiles(value_delta), tiles(attended_rows), tiles(grad_projected)))
    layer_out = jnp.concatenate(outs_forward, axis=0)
    tokens_grad = jnp.concatenate(outs_grad, axis=0)
    return (layer_out, tokens_grad, sums[0], sums[1], sums[2], sums[3])
```

```python
import functools

import jax
import jax.numpy as jnp
from jax import lax
from jax.experimental import pallas as pl
from jax.experimental.pallas import tpu as pltpu
from jax.sharding import PartitionSpec as P

EPS = 1e-06
ROPE_BASE = 10000.0
Q_FACTOR = 0.0625
WINDOW = 1024
F32 = jnp.float32
BF16 = jnp.bfloat16
MESH = pl.DeviceIdType.MESH
VMEM_LIMIT = 64 * 1024 * 1024 - 512 * 1024

D = 2560
ROWS = 384
NOTE_ROWS = 16
UNIT = 2 * ROWS + NOTE_ROWS


def place():
    y = lax.axis_index("fsdp")
    c = lax.axis_index("ctx")
    j = lax.rem(c, 2)
    zx = lax.div(c, 2)
    return y, lax.div(zx, 4), lax.rem(zx, 4), j


def dev(y, z, x, j):
    return (y, (z * 4 + x) * 2 + j)


def up(a, n=1):
    return lax.rem(a + n, 4)


def remote(src, dst, ss, rs, device):
    return pltpu.make_async_remote_copy(
        src_ref=src, dst_ref=dst, send_sem=ss, recv_sem=rs, device_id=device, device_id_type=MESH
    )


def meet(devices):
    barrier = pltpu.get_barrier_semaphore()
    for device in devices:
        pl.semaphore_signal(barrier, inc=1, device_id=device, device_id_type=MESH)
    pl.semaphore_wait(barrier, len(devices))


def rows_at(start, size, unit=16):
    return pl.ds(pl.multiple_of(start, unit), size)


def vmem(n):
    return [pl.BlockSpec(memory_space=pltpu.VMEM)] * n


def comm_call(kernel, name, cid, out_shape, scratch, n_in):
    return pl.pallas_call(
        kernel,
        name=name,
        out_shape=out_shape,
        in_specs=vmem(n_in),
        out_specs=jax.tree.map(lambda _: pl.BlockSpec(memory_space=pltpu.VMEM), out_shape),
        scratch_shapes=scratch,
        compiler_params=pltpu.CompilerParams(
            collective_id=cid, has_side_effects=True, vmem_limit_bytes=VMEM_LIMIT
        ),
    )


def sds(shape, dtype):
    return jax.ShapeDtypeStruct(shape, dtype)


DMA = pltpu.SemaphoreType.DMA


class RingGather:
    def __init__(self, me, plus, minus, region, half, ss, rs, index):
        self.me, self.plus, self.minus = me, plus, minus
        self.region, self.half, self.ss, self.rs, self.index = region, half, ss, rs, index

    def _copy(self, ref, k, device):
        at = self.index + (k,)
        return remote(ref, ref, self.ss.at[at], self.rs.at[at], device)

    def start(self):
        self._copy(self.region(self.me), 0, self.plus).start()
        self._copy(self.region(self.me), 1, self.minus).start()

    def forward(self):
        left, right = up(self.me, 3), up(self.me, 1)
        self._copy(self.region(left), 0, self.plus).wait_recv()
        self._copy(self.half(left, 0), 2, self.plus).start()
        self._copy(self.region(right), 1, self.minus).wait_recv()
        self._copy(self.half(right, 1), 3, self.minus).start()

    def finish(self):
        far = up(self.me, 2)
        self._copy(self.half(far, 0), 2, self.plus).wait_recv()
        self._copy(self.half(far, 1), 3, self.minus).wait_recv()

    def drain(self):
        self._copy(self.region(self.me), 0, self.plus).wait_send()
        self._copy(self.region(self.me), 1, self.minus).wait_send()
        self._copy(self.half(up(self.me, 3), 0), 2, self.plus).wait_send()
        self._copy(self.half(up(self.me, 1), 1), 3, self.minus).wait_send()


def gather_kernel(n_ref, wq, wk, wv, n2, w, lsem, nsem, ysend, yrecv, gsend, grecv):
    y, z, x, j = place()
    partner = dev(y, z, x, 1 - j)
    xp, xm = dev(y, z, up(x), j), dev(y, z, up(x, 3), j)
    zp, zm = dev(y, up(z), x, j), dev(y, up(z, 3), x, j)
    ys = [dev(up(y, r), z, x, j) for r in (1, 2, 3)]
    own = rows_at(640 * y, 640)
    local = []
    for b in range(8):
        if b < 4:
            src = wq.at[:, pl.ds(pl.multiple_of(512 * j + 128 * b, 128), 128)]
        elif b < 6:
            src = wk.at[:, pl.ds(pl.multiple_of(256 * j + 128 * (b - 4), 128), 128)]
        else:
            src = wv.at[:, pl.ds(pl.multiple_of(256 * j + 128 * (b - 6), 128), 128)]
        local.append(pltpu.make_async_copy(src, w.at[b, own], lsem.at[b]))
    local.append(pltpu.make_async_copy(n_ref, n2.at[j], lsem.at[8]))
    for cp in local:
        cp.start()
    meet([partner, xp, xm, zp, zm] + ys)
    for cp in local[:8]:
        cp.wait()

    def piece_q(yy):
        return w.at[x, rows_at(640 * yy + 160 * z, 160)]

    def piece_k(yy):
        return w.at[4 + z, rows_at(640 * yy + 160 * x, 160)]

    first = []
    for r in range(3):
        for f, piece in enumerate((piece_q, piece_k)):
            cp = remote(piece(y), piece(y), ysend.at[f, r], yrecv.at[f, r], ys[r])
            cp.start()
            first.append((cp, f, r, piece))
    swap = remote(n_ref, n2.at[j], nsem.at[0], nsem.at[1], partner)
    swap.start()

    def ring(f, stage, r):
        yy = up(y, 3 - r)
        if f == 0 and stage == 0:
            region = lambda m: w.at[m, rows_at(640 * yy + 160 * z, 160)]
            half = lambda m, h: w.at[m, rows_at(640 * yy + 160 * z + 80 * h, 80)]
        elif f == 0:
            region = lambda m: w.at[pl.ds(0, 4), rows_at(640 * yy + 160 * m, 160)]
            half = lambda m, h: w.at[pl.ds(2 * h, 2), rows_at(640 * yy + 160 * m, 160)]
        elif stage == 0:
            region = lambda m: w.at[4 + m, rows_at(640 * yy + 160 * x, 160)]
            half = lambda m, h: w.at[4 + m, rows_at(640 * yy + 160 * x + 80 * h, 80)]
        else:
            region = lambda m: w.at[pl.ds(4, 4), rows_at(640 * yy + 160 * m, 160)]
            half = lambda m, h: w.at[pl.ds(4 + 2 * h, 2), rows_at(640 * yy + 160 * m, 160)]
        on_x = (f + stage) % 2 == 0
        me, plus, minus = (x, xp, xm) if on_x else (z, zp, zm)
        return RingGather(me, plus, minus, region, half, gsend, grecv, (f, stage, r))

    rings = [[[ring(f, s, r) for r in range(3)] for s in range(2)] for f in range(2)]
    for cp, f, r, piece in first:
        yy = up(y, 3 - r)
        remote(piece(yy), piece(yy), ysend.at[f, r], yrecv.at[f, r], ys[r]).wait_recv()
        rings[f][0][r].start()
    for r in range(3):
        for f in range(2):
            rings[f][0][r].forward()
    for r in range(3):
        for f in range(2):
            rings[f][0][r].finish()
            rings[f][1][r].start()
    for r in range(3):
        for f in range(2):
            rings[f][1][r].forward()
    for r in range(3):
        for f in range(2):
            rings[f][1][r].finish()
    for r in range(3):
        for f in range(2):
            rings[f][0][r].drain()
            rings[f][1][r].drain()
    for cp, f, r, piece in first:
        cp.wait_send()
    swap.wait()
    local[8].wait()


def gather(noted, wq, wk, wv):
    return comm_call(
        gather_kernel,
        "gather_weights",
        0,
        (sds((2, ROWS + NOTE_ROWS, D), BF16), sds((8, D, 128), BF16)),
        [
            DMA((9,)),
            DMA((2,)),
            DMA((2, 3)),
            DMA((2, 3)),
            DMA((2, 2, 3, 4)),
            DMA((2, 2, 3, 4)),
        ],
        4,
    )(noted, wq, wk, wv)


def project_kernel(n2, w, cos, sin, gains, q_out, unit, raw_out):
    n = pl.program_id(0)
    rows = n2[:, :ROWS, :].reshape(2 * ROWS, D)
    weight = jnp.concatenate([w[0], w[1]], axis=-1)
    acc = jnp.dot(rows, weight, preferred_element_type=F32)

    def rotated(gain, factor):
        scale = lax.rsqrt(jnp.mean(acc * acc, axis=-1, keepdims=True) + EPS)
        normed = acc * scale * gain
        a, b = normed[:, :128], normed[:, 128:]
        c, s = cos[...], sin[...]
        return (jnp.concatenate([a * c - b * s, b * c + a * s], axis=-1) * factor).astype(BF16)

    @pl.when(n < 3)
    def _():
        raw_out[0] = acc

    @pl.when(n < 2)
    def _():
        q_out[0] = rotated(gains[0:1, :], Q_FACTOR)

    @pl.when(n == 2)
    def _():
        unit[0 : 2 * ROWS, 0:256] = rotated(gains[1:2, :], 1.0)

    @pl.when(n == 3)
    def _():
        unit[0 : 2 * ROWS, 256:512] = acc.astype(BF16)
        unit[2 * ROWS : UNIT, :] = n2[0, ROWS:, 0:512] + n2[1, ROWS:, 0:512]


def project(n2, w, cos, sin, gains):
    return pl.pallas_call(
        project_kernel,
        name="project",
        grid=(4,),
        in_specs=[
            pl.BlockSpec((2, ROWS + NOTE_ROWS, D), lambda n: (0, 0, 0)),
            pl.BlockSpec((2, D, 128), lambda n: (n, 0, 0)),
            pl.BlockSpec((2 * ROWS, 128), lambda n: (0, 0)),
            pl.BlockSpec((2 * ROWS, 128), lambda n: (0, 0)),
            pl.BlockSpec((8, 256), lambda n: (0, 0)),
        ],
        out_specs=[
            pl.BlockSpec((1, 2 * ROWS, 256), lambda n: (jnp.minimum(n, 1), 0, 0)),
            pl.BlockSpec((UNIT, 512), lambda n: (0, 0)),
            pl.BlockSpec((1, 2 * ROWS, 256), lambda n: (jnp.minimum(n, 2), 0, 0)),
        ],
        out_shape=[
            sds((2, 2 * ROWS, 256), BF16),
            sds((UNIT, 512), BF16),
            sds((3, 2 * ROWS, 256), F32),
        ],
        compiler_params=pltpu.CompilerParams(vmem_limit_bytes=VMEM_LIMIT),
    )(n2, w, cos, sin, gains)


HALO_CHUNKS = 7
HALO_ROWS = UNIT // HALO_CHUNKS


def halo_kernel(unit, wo_own, w, halo, wo, wfull, hsend, hrecv, osend, orecv, lsem, wsem):
    y, z, x, j = place()
    partner = dev(y, z, x, 1 - j)
    xp, xm = dev(y, z, up(x), j), dev(y, z, up(x, 3), j)
    zp, zm = dev(y, up(z), x, j), dev(y, up(z, 3), x, j)
    yp, ym = dev(up(y), z, x, j), dev(up(y, 3), z, x, j)
    wcopy = pltpu.make_async_copy(w, wfull.at[j], lsem.at[0])
    ocopy = pltpu.make_async_copy(wo_own, wo.at[y], lsem.at[1])
    wcopy.start()
    ocopy.start()
    meet([partner, xp, xm, zp, zm, yp, ym])

    def rows(k):
        return rows_at(k * HALO_ROWS, HALO_ROWS)

    def shift(k):
        return remote(unit.at[rows(k)], halo.at[3, rows(k)], hsend.at[0, k], hrecv.at[0, k], zp)

    def right(src, k):
        return remote(src.at[rows(k)], halo.at[0, rows(k)], hsend.at[1, k], hrecv.at[1, k], xp)

    def left(src, k):
        return remote(src.at[rows(k)], halo.at[2, rows(k)], hsend.at[2, k], hrecv.at[2, k], xm)

    def far_right(k):
        return remote(
            halo.at[0, rows(k)], halo.at[1, rows(k)], hsend.at[3, k], hrecv.at[3, k], xp
        )

    def far_left(k):
        return remote(
            halo.at[2, rows(k)], halo.at[1, rows(k)], hsend.at[4, k], hrecv.at[3, k], xm
        )

    before = halo.at[3]
    inner = jnp.logical_and(x > 0, x < 3)

    @pl.loop(0, HALO_CHUNKS)
    def _(k):
        shift(k).start()

        @pl.when(x < 3)
        def _():
            right(unit, k).start()

        @pl.when(x == 0)
        def _():
            left(unit, k).start()

    ocopy.wait()
    ring = RingGather(
        y,
        yp,
        ym,
        lambda m: wo.at[m, j],
        lambda m, h: wo.at[m, j, pl.ds(64 * h, 64)],
        osend,
        orecv,
        (0,),
    )
    ring.start()
    swap = remote(w, wfull.at[j], wsem.at[0], wsem.at[1], partner)
    swap.start()

    @pl.loop(0, HALO_CHUNKS)
    def _(k):
        shift(k).wait_recv()

        @pl.when(x == 3)
        def _():
            right(before, k).start()

        @pl.when(x > 0)
        def _():
            left(before, k).start()

        right(unit, k).wait_recv()

        @pl.when(inner)
        def _():
            far_right(k).start()

        @pl.when(k > 0)
        def _():
            left(unit, k - 1).wait_recv()

            @pl.when(inner)
            def _():
                far_left(k - 1).start()

    left(unit, HALO_CHUNKS - 1).wait_recv()

    @pl.when(inner)
    def _():
        far_left(HALO_CHUNKS - 1).start()

    ring.forward()
    share = []
    for n, m in enumerate((up(y, 3), up(y, 1), up(y, 2))):
        if n == 2:
            ring.finish()
        cp = remote(
            wo.at[m, j], wo.at[m, j], osend.at[1, n], orecv.at[1, n], partner
        )
        cp.start()
        share.append(cp)
    for n, m in enumerate((up(y, 3), up(y, 1), up(y, 2))):
        remote(
            wo.at[m, 1 - j], wo.at[m, 1 - j], osend.at[1, n], orecv.at[1, n], partner
        ).wait_recv()
    for cp in share:
        cp.wait_send()
    ring.drain()

    @pl.loop(0, HALO_CHUNKS)
    def _(k):
        far_right(k).wait_recv()
        shift(k).wait_send()
        right(unit, k).wait_send()
        left(unit, k).wait_send()

        @pl.when(inner)
        def _():
            far_right(k).wait_send()
            far_left(k).wait_send()

    swap.wait()
    wcopy.wait()


def exchange_halo(unit, wo_own, w):
    return comm_call(
        halo_kernel,
        "exchange_halo",
        1,
        (
            sds((4, UNIT, 512), BF16),
            sds((4, 2, 128, D), BF16),
            sds((2, 8, D, 128), BF16),
        ),
        [
            DMA((5, HALO_CHUNKS)),
            DMA((4, HALO_CHUNKS)),
            DMA((2, 4)),
            DMA((2, 4)),
            DMA((2,)),
            DMA((2,)),
        ],
        3,
    )(unit, wo_own, w)


KEYS = 1280


def window_of(unit, halo, s, first, last):
    parts = []
    for d in (4, 3, 2, 1, 0):
        for i in range(2):
            at = rows_at(i * ROWS + s * 128, 128)
            if d == 0:
                parts.append(unit[at, first:last])
            else:
                parts.append(halo[d - 1, at, first:last])
    return jnp.concatenate(parts, axis=0)


def forward_kernel(q, unit, halo, base, attended, soft):
    s = pl.program_id(0)
    keys = window_of(unit, halo, s, 0, 256)
    values = window_of(unit, halo, s, 256, 512)
    lanes = pl.ds(pl.multiple_of(s * 128, 128), 128)
    notes = []
    for d in (4, 3, 2, 1, 0):
        block = unit[2 * ROWS :, lanes] if d == 0 else halo[d - 1, 2 * ROWS :, lanes]
        block = block.astype(F32)
        notes.extend([block[0:1], block[8:9]])
    key_docs = jnp.concatenate(notes, axis=-1)
    query_docs = jnp.concatenate(
        [jnp.transpose(jnp.broadcast_to(note, (128, 128))) for note in notes[8:]], axis=0
    )
    query_docs = jnp.concatenate([query_docs] * (KEYS // 128), axis=-1)
    key_at = lax.broadcasted_iota(jnp.int32, (256, KEYS), 1) - WINDOW
    query_at = lax.broadcasted_iota(jnp.int32, (256, KEYS), 0)
    start = base[0]
    allowed = (
        (query_docs == key_docs)
        & (key_at <= query_at)
        & (key_at > query_at - WINDOW)
        & (key_at + start >= 0)
    )
    bias = jnp.where(allowed, 0.0, -1e30)
    for h in range(2):
        rows = q[h, :, 0].reshape(256, 256)
        scores = lax.dot_general(
            rows, keys, (((1,), (1,)), ((), ())), preferred_element_type=F32
        )
        masked = jnp.where(bias < 0.0, -1e30, scores)
        highest = jnp.max(masked, axis=-1, keepdims=True)
        raised = jnp.exp(masked - highest)
        weights = (raised / jnp.sum(raised, axis=-1, keepdims=True)).astype(BF16)
        soft[0, 256 * h : 256 * h + 256, :] = weights
        out = jnp.dot(weights, values, preferred_element_type=F32).astype(BF16)
        attended[:, 0, :, 256 * h : 256 * h + 256] = out.reshape(2, 128, 256)


def attend_forward(q, unit, halo, base):
    return pl.pallas_call(
        forward_kernel,
        name="attend_forward",
        grid=(3,),
        in_specs=[
            pl.BlockSpec((2, 2, 1, 128, 256), lambda s: (0, 0, s, 0, 0)),
            pl.BlockSpec((UNIT, 512), lambda s: (0, 0)),
            pl.BlockSpec((4, UNIT, 512), lambda s: (0, 0, 0)),
            pl.BlockSpec(memory_space=pltpu.SMEM),
        ],
        out_specs=[
            pl.BlockSpec((2, 1, 128, 512), lambda s: (0, s, 0, 0)),
            pl.BlockSpec((1, 512, KEYS), lambda s: (s, 0, 0)),
        ],
        out_shape=[sds((2, 3, 128, 512), BF16), sds((3, 512, KEYS), BF16)],
        compiler_params=pltpu.CompilerParams(vmem_limit_bytes=VMEM_LIMIT),
    )(q.reshape(2, 2, 3, 128, 256), unit, halo, base)


def backward_kernel(q, unit, halo, soft, grad, raw, cos, sin, gains, delta_out, own, parts):
    s = pl.program_id(0)
    keys = window_of(unit, halo, s, 0, 256)
    values = window_of(unit, halo, s, 256, 512)
    grads = jnp.concatenate(
        [grad[:, 0, :, 256 * h : 256 * h + 256].reshape(256, 256) for h in range(2)], axis=0
    )
    weights = soft[0]
    value_part = lax.dot_general(
        weights, grads, (((0,), (0,)), ((), ())), preferred_element_type=F32
    )

    def emit(part, first):
        for n, d in enumerate((4, 3, 2, 1, 0)):
            for i in range(2):
                piece = part[256 * n + 128 * i : 256 * n + 128 * i + 128]
                if d == 0:
                    own[i, 0, :, first : first + 256] = piece
                else:
                    parts[d - 1, i, 0, :, first : first + 256] = piece.astype(BF16)

    emit(value_part, 256)
    grad_weights = lax.dot_general(
        grads, values, (((1,), (1,)), ((), ())), preferred_element_type=F32
    )
    wide = weights.astype(F32)
    moved = wide * grad_weights
    dots = jnp.sum(moved, axis=-1, keepdims=True)
    score_grads = (moved - wide * dots).astype(BF16)
    grad_queries = jnp.dot(score_grads, keys, preferred_element_type=F32)
    queries = q[:, :, 0].reshape(512, 256)
    emit(
        lax.dot_general(
            score_grads, queries, (((0,), (0,)), ((), ())), preferred_element_type=F32
        ),
        0,
    )
    gain = gains[0:1, :]
    c = cos[:, 0].reshape(256, 128)
    sn = sin[:, 0].reshape(256, 128)
    for h in range(2):
        back = map_back(
            grad_queries[256 * h : 256 * h + 256],
            raw[h, :, 0].reshape(256, 256),
            c,
            sn,
            gain,
            Q_FACTOR,
        )
        delta_out[:, 0, :, 256 * h : 256 * h + 256] = back.astype(BF16).reshape(2, 128, 256)


def map_back(upstream, raw, c, s, gain, factor):
    a, b = upstream[:, :128] * factor, upstream[:, 128:] * factor
    turned = jnp.concatenate([a * c + b * s, b * c - a * s], axis=-1) * gain
    scale = lax.rsqrt(jnp.mean(raw * raw, axis=-1, keepdims=True) + EPS)
    inner = jnp.mean(turned * raw, axis=-1, keepdims=True)
    return scale * turned - raw * (scale * scale * scale * inner)


def attend_backward(q, unit, halo, soft, grad, raw, cos, sin, gains):
    row_block = pl.BlockSpec((2, 1, 128, 512), lambda s: (0, s, 0, 0))
    angle = pl.BlockSpec((2, 1, 128, 128), lambda s: (0, s, 0, 0))
    head_block = pl.BlockSpec((2, 2, 1, 128, 256), lambda s: (0, 0, s, 0, 0))
    return pl.pallas_call(
        backward_kernel,
        name="attend_backward",
        grid=(3,),
        in_specs=[
            head_block,
            pl.BlockSpec((UNIT, 512), lambda s: (0, 0)),
            pl.BlockSpec((4, UNIT, 512), lambda s: (0, 0, 0)),
            pl.BlockSpec((1, 512, KEYS), lambda s: (s, 0, 0)),
            row_block,
            head_block,
            angle,
            angle,
            pl.BlockSpec((8, 256), lambda s: (0, 0)),
        ],
        out_specs=[
            row_block,
            row_block,
            pl.BlockSpec((4, 2, 1, 128, 512), lambda s: (0, 0, s, 0, 0)),
        ],
        out_shape=[
            sds((2, 3, 128, 512), BF16),
            sds((2, 3, 128, 512), F32),
            sds((4, 2, 3, 128, 512), BF16),
        ],
        compiler_params=pltpu.CompilerParams(vmem_limit_bytes=VMEM_LIMIT),
    )(
        q.reshape(2, 2, 3, 128, 256),
        unit,
        halo,
        soft,
        grad.reshape(2, 3, 128, 512),
        raw.reshape(3, 2, 3, 128, 256),
        cos.reshape(2, 3, 128, 128),
        sin.reshape(2, 3, 128, 128),
        gains,
    )


def swap_kernel(count, *refs):
    halves = refs[:1]
    whole = refs[1:count]
    outs = refs[count : 2 * count]
    lsem, ssem, rsem = refs[2 * count :]
    y, z, x, j = place()
    partner = dev(y, z, x, 1 - j)
    local = []
    for n in range(count):
        src = halves[0].at[j] if n < 1 else whole[n - 1]
        cp = pltpu.make_async_copy(src, outs[n].at[j], lsem.at[n])
        cp.start()
        local.append(cp)
    meet([partner])
    sent = []
    for n in range(count):
        src = halves[0].at[1 - j] if n < 1 else whole[n - 1]
        cp = remote(src, outs[n].at[j], ssem.at[n], rsem.at[n], partner)
        cp.start()
        sent.append(cp)
    for cp in local:
        cp.wait()
    for cp in sent:
        cp.wait()


def swap(name, cid, halves, *whole):
    count = 1 + len(whole)
    shapes = [sds(halves.shape, halves.dtype)] + [sds((2,) + w.shape, w.dtype) for w in whole]
    return comm_call(
        functools.partial(swap_kernel, count),
        name,
        cid,
        shapes,
        [DMA((count,)), DMA((count,)), DMA((count,))],
        count,
    )(halves, *whole)


def output_kernel(att, wo, tok, cot, gain, layer_out, gp, ga, proj, up_buf):
    left, right = att[0], att[1]
    for n in range(5):
        cols = slice(512 * n, 512 * n + 512)
        proj[:, cols] = jnp.dot(left, wo[0:512, cols], preferred_element_type=F32) + jnp.dot(
            right, wo[512:1024, cols], preferred_element_type=F32
        )

    @pl.loop(0, ROWS // 16)
    def _(k):
        at = rows_at(k * 16, 16)
        p = proj[at, :]
        g = gain[...]
        scale = lax.rsqrt(jnp.mean(p * p, axis=-1, keepdims=True) + EPS)
        layer_out[at, :] = (tok[at, :].astype(F32) + p * scale * g).astype(BF16)
        h = cot[at, :].astype(F32) * g
        inner = jnp.mean(h * p, axis=-1, keepdims=True)
        gp[at, :] = (scale * h - p * (scale * scale * scale * inner)).astype(BF16)

    upstream = gp[...]
    for half in range(2):
        ga[half] = lax.dot_general(
            upstream,
            wo[512 * half : 512 * half + 512, :],
            (((1,), (1,)), ((), ())),
            preferred_element_type=F32,
        ).astype(BF16)


def output_stage(att, wo, tok, cot, gain):
    return pl.pallas_call(
        output_kernel,
        name="output_stage",
        in_specs=vmem(5),
        out_specs=vmem(3),
        out_shape=[sds((ROWS, D), BF16), sds((ROWS, D), BF16), sds((2, ROWS, 512), BF16)],
        scratch_shapes=[pltpu.VMEM((ROWS, D), F32), pltpu.VMEM((8, 128), F32)],
        compiler_params=pltpu.CompilerParams(vmem_limit_bytes=VMEM_LIMIT),
    )(att, wo, tok, cot, gain)


CHUNKS = 6


def return_kernel(parts, own, total, relay, near, after, relayed, summed, bsum, ssem, rsem):
    y, z, x, j = place()
    xp, xm = dev(y, z, up(x), j), dev(y, z, up(x, 3), j)
    zp, zm = dev(y, up(z), x, j), dev(y, up(z, 3), x, j)
    meet([xp, xm, zp, zm])
    inner = jnp.logical_and(x > 0, x < 3)
    low = x < 2

    def relay_left(k):
        return remote(parts.at[1, k], relay.at[0, k], ssem.at[0, k], rsem.at[0, k], xm)

    def relay_right(k):
        return remote(parts.at[1, k], relay.at[1, k], ssem.at[1, k], rsem.at[1, k], xp)

    def to_left(src, k):
        return remote(src.at[k], near.at[0, k], ssem.at[2, k], rsem.at[2, k], xm)

    def to_right(src, k):
        return remote(src.at[k], near.at[1, k], ssem.at[3, k], rsem.at[3, k], xp)

    def back(k):
        return remote(bsum.at[k], after.at[k], ssem.at[4, k], rsem.at[4, k], zm)

    @pl.loop(0, CHUNKS)
    def _(k):
        @pl.when(low)
        def _():
            relay_right(k).start()

        @pl.when(jnp.logical_not(low))
        def _():
            relay_left(k).start()

        @pl.when(jnp.logical_not(inner))
        def _():
            to_left(parts.at[0], k).start()
            to_right(parts.at[2], k).start()

    @pl.when(inner)
    def _():
        @pl.loop(0, CHUNKS)
        def _(k):
            relay_left(k).wait_recv()
            relayed[0, k] = (parts[0, k].astype(F32) + relay[0, k].astype(F32)).astype(BF16)
            to_left(relayed.at[0], k).start()
            relay_right(k).wait_recv()
            relayed[1, k] = (parts[2, k].astype(F32) + relay[1, k].astype(F32)).astype(BF16)
            to_right(relayed.at[1], k).start()

    @pl.loop(0, CHUNKS)
    def _(k):
        to_left(parts.at[0], k).wait_recv()
        to_right(parts.at[2], k).wait_recv()
        from_right = near[0, k].astype(F32)
        from_left = near[1, k].astype(F32)
        zero = jnp.zeros_like(from_left)
        near_a = jnp.where(x < 3, from_right, zero) + jnp.where(x == 0, from_left, zero)
        near_b = jnp.where(x == 3, from_right, zero) + jnp.where(x > 0, from_left, zero)
        summed[k] = near_a
        bsum[k] = (parts[3, k].astype(F32) + near_b).astype(BF16)
        back(k).start()

    @pl.loop(0, CHUNKS)
    def _(k):
        back(k).wait_recv()
        total[k] = own[k] + summed[k] + after[k].astype(F32)

    @pl.loop(0, CHUNKS)
    def _(k):
        @pl.when(low)
        def _():
            relay_right(k).wait_send()

        @pl.when(jnp.logical_not(low))
        def _():
            relay_left(k).wait_send()

        to_left(parts.at[0], k).wait_send()
        to_right(parts.at[2], k).wait_send()
        back(k).wait_send()


def return_grads(parts, own):
    block = (CHUNKS, 128, 512)
    return comm_call(
        return_kernel,
        "return_grads",
        2,
        sds(block, F32),
        [
            pltpu.VMEM((2,) + block, BF16),
            pltpu.VMEM((2,) + block, BF16),
            pltpu.VMEM(block, BF16),
            pltpu.VMEM((2,) + block, BF16),
            pltpu.VMEM(block, F32),
            pltpu.VMEM(block, BF16),
            DMA((5, CHUNKS)),
            DMA((5, CHUNKS)),
        ],
        2,
    )(parts.reshape((4,) + block), own.reshape(block))


def in_grads_kernel(n2, total, raw, cos, sin, gains, qd, gq, gkv, kvd):
    @pl.when(pl.program_id(0) == 0)
    def _():
        kd = map_back(total[:, :256], raw[0], cos[...], sin[...], gains[1:2, :], 1.0)
        kvd[:, :256] = kd.astype(BF16)
        kvd[:, 256:] = total[:, 256:].astype(BF16)

    rows = n2[:, :ROWS, :].reshape(2 * ROWS, 640)
    for half in range(2):
        rhs_q = qd[:, 256 * half : 256 * half + 256]
        rhs_kv = jnp.concatenate(
            [kvd[:, 128 * half : 128 * half + 128], kvd[:, 256 + 128 * half : 384 + 128 * half]],
            axis=-1,
        )
        for rhs, out in ((rhs_q, gq), (rhs_kv, gkv)):
            term = lax.dot_general(
                rows, rhs, (((0,), (0,)), ((), ())), preferred_element_type=F32
            )
            out[half, 0] = term.astype(BF16).reshape(4, 160, 256)


def in_grads(n2, total, raw, cos, sin, gains, qd):
    grads = pl.BlockSpec((2, 1, 4, 160, 256), lambda n: (0, n, 0, 0, 0))
    return pl.pallas_call(
        in_grads_kernel,
        name="in_grads",
        grid=(4,),
        in_specs=[
            pl.BlockSpec((2, ROWS + NOTE_ROWS, 640), lambda n: (0, 0, n)),
            pl.BlockSpec((2 * ROWS, 512), lambda n: (0, 0)),
            pl.BlockSpec((1, 2 * ROWS, 256), lambda n: (2, 0, 0)),
            pl.BlockSpec((2 * ROWS, 128), lambda n: (0, 0)),
            pl.BlockSpec((2 * ROWS, 128), lambda n: (0, 0)),
            pl.BlockSpec((8, 256), lambda n: (0, 0)),
            pl.BlockSpec((2 * ROWS, 512), lambda n: (0, 0)),
        ],
        out_specs=[grads, grads, pl.BlockSpec((2 * ROWS, 512), lambda n: (0, 0))],
        out_shape=[
            sds((2, 4, 4, 160, 256), BF16),
            sds((2, 4, 4, 160, 256), BF16),
            sds((2 * ROWS, 512), BF16),
        ],
        compiler_params=pltpu.CompilerParams(vmem_limit_bytes=VMEM_LIMIT),
    )(n2, total, raw, cos, sin, gains, qd)


def out_grads_kernel(att, gp2, out):
    term = lax.dot_general(
        att[...],
        gp2[...].reshape(2 * ROWS, 640),
        (((0,), (0,)), ((), ())),
        preferred_element_type=F32,
    )
    out[0] = term.astype(BF16).reshape(2, 4, 64, 640)


def out_grads(att, gp2):
    return pl.pallas_call(
        out_grads_kernel,
        name="out_grads",
        grid=(4,),
        in_specs=[
            pl.BlockSpec((2 * ROWS, 512), lambda n: (0, 0)),
            pl.BlockSpec((2, ROWS, 640), lambda n: (0, 0, n)),
        ],
        out_specs=pl.BlockSpec((1, 2, 4, 64, 640), lambda n: (n, 0, 0, 0, 0)),
        out_shape=sds((4, 2, 4, 64, 640), BF16),
        compiler_params=pltpu.CompilerParams(vmem_limit_bytes=VMEM_LIMIT),
    )(att, gp2)


def input_kernel(dq, dkv, w, tok, cot, gain, out, acc):
    n = pl.program_id(0)
    total = None
    for half in range(2):
        lhs = jnp.concatenate([dq[half], dkv[half]], axis=-1)
        rhs = jnp.concatenate([w[half, b] for b in range(8)], axis=-1)
        term = lax.dot_general(lhs, rhs, (((1,), (1,)), ((), ())), preferred_element_type=F32)
        total = term if total is None else total + term
    acc[n] = total

    @pl.when(n == pl.num_programs(0) - 1)
    def _():
        @pl.loop(0, ROWS // 16)
        def _(k):
            at = rows_at(k * 16, 16)
            t = tok[at, :].astype(F32)
            grad = jnp.concatenate([acc[m, at, :] for m in range(5)], axis=-1)
            h = grad * gain[...]
            scale = lax.rsqrt(jnp.mean(t * t, axis=-1, keepdims=True) + EPS)
            inner = jnp.mean(h * t, axis=-1, keepdims=True)
            back = scale * h - t * (scale * scale * scale * inner)
            out[at, :] = (cot[at, :].astype(F32) + back).astype(BF16)


def input_stage(dq, dkv, wfull, tok, cot, gain):
    return pl.pallas_call(
        input_kernel,
        name="input_stage",
        grid=(5,),
        in_specs=[
            pl.BlockSpec((2, ROWS, 512), lambda n: (0, 0, 0)),
            pl.BlockSpec((2, ROWS, 512), lambda n: (0, 0, 0)),
            pl.BlockSpec((2, 8, 512, 128), lambda n: (0, 0, n, 0)),
            pl.BlockSpec((ROWS, D), lambda n: (0, 0)),
            pl.BlockSpec((ROWS, D), lambda n: (0, 0)),
            pl.BlockSpec((1, D), lambda n: (0, 0)),
        ],
        out_specs=pl.BlockSpec((ROWS, D), lambda n: (0, 0)),
        out_shape=sds((ROWS, D), BF16),
        scratch_shapes=[pltpu.VMEM((5, ROWS, 512), F32)],
        compiler_params=pltpu.CompilerParams(vmem_limit_bytes=VMEM_LIMIT),
    )(dq, dkv, wfull, tok, cot, gain)


def add_into(ref, at, other):
    ref[at] = (ref[at].astype(F32) + other.astype(F32)).astype(BF16)


class RingReduce:
    def __init__(self, me, plus, minus, data, pick, half, relay, recv, ss, rs, index):
        self.me, self.plus, self.minus = me, plus, minus
        self.data, self.pick, self.half = data, pick, half
        self.relay, self.recv, self.ss, self.rs, self.index = relay, recv, ss, rs, index

    def _copy(self, src, dst, k, device):
        at = self.index + (k,)
        return remote(src, dst, self.ss.at[at], self.rs.at[at], device)

    def _first(self):
        far = up(self.me, 2)
        return (
            self._copy(self.data.at[self.half(far, 0)], self.relay.at[0], 0, self.plus),
            self._copy(self.data.at[self.half(far, 1)], self.relay.at[1], 1, self.minus),
        )

    def _second(self):
        right, left = up(self.me, 1), up(self.me, 3)
        return (
            self._copy(self.data.at[self.pick(right)], self.recv.at[0], 2, self.plus),
            self._copy(self.data.at[self.pick(left)], self.recv.at[1], 3, self.minus),
        )

    def start(self):
        for cp in self._first():
            cp.start()

    def forward(self):
        a, b = self._first()
        c, d = self._second()
        a.wait_recv()
        add_into(self.data, self.half(up(self.me, 1), 0), self.relay[0])
        c.start()
        b.wait_recv()
        add_into(self.data, self.half(up(self.me, 3), 1), self.relay[1])
        d.start()

    def finish(self):
        c, d = self._second()
        c.wait_recv()
        d.wait_recv()
        return (
            self.data[self.pick(self.me)].astype(F32)
            + self.recv[0].astype(F32)
            + self.recv[1].astype(F32)
        )

    def drain(self):
        for cp in self._first() + self._second():
            cp.wait_send()


def reduce_kernel(
    gq, gkv, go, oq, okv, oo,
    q_relay, q_recv, q_mid, q_relay2, q_recv2, q_end, q_land,
    k_relay, k_recv, k_mid, k_relay2, k_recv2, k_end, k_land,
    o_relay, o_recv, o_mid, o_relay2, o_recv2, o_end, o_land,
    ss, rs, ls, lr, lc,
):
    y, z, x, j = place()
    partner = dev(y, z, x, 1 - j)
    xp, xm = dev(y, z, up(x), j), dev(y, z, up(x, 3), j)
    zp, zm = dev(y, up(z), x, j), dev(y, up(z, 3), x, j)
    yp, ym = dev(up(y), z, x, j), dev(up(y, 3), z, x, j)
    yfar = [dev(up(y, r), z, x, i) for r in (1, 2, 3) for i in (0, 1)]
    zfar = [dev(y, up(z, r), x, i) for r in (1, 2, 3) for i in (0, 1)]
    meet([partner, xp, xm] + yfar + zfar)
    every = slice(None)
    q1 = RingReduce(
        x, xp, xm, gq, lambda m: (every, every, m), lambda m, h: (h, every, m),
        q_relay, q_recv, ss, rs, (0, 0),
    )
    k1 = RingReduce(
        z, zp, zm, gkv, lambda m: (every, m), lambda m, h: (h, m),
        k_relay, k_recv, ss, rs, (1, 0),
    )
    o1 = RingReduce(
        y, yp, ym, go, lambda m: (m,), lambda m, h: (m, h),
        o_relay, o_recv, ss, rs, (2, 0),
    )
    q2 = RingReduce(
        z, zp, zm, q_mid, lambda m: (every, m), lambda m, h: (h, m),
        q_relay2, q_recv2, ss, rs, (0, 1),
    )
    k2 = RingReduce(
        x, xp, xm, k_mid, lambda m: (every, m), lambda m, h: (h, m),
        k_relay2, k_recv2, ss, rs, (1, 1),
    )
    o2 = RingReduce(
        x, xp, xm, o_mid, lambda m: (every, m), lambda m, h: (h, m),
        o_relay2, o_recv2, ss, rs, (2, 1),
    )
    firsts, seconds = (o1, k1, q1), (o2, k2, q2)
    mids, ends = (o_mid, k_mid, q_mid), (o_end, k_end, q_end)
    for ring in firsts:
        ring.start()
    for ring in firsts:
        ring.forward()
    for ring, mid, after in zip(firsts, mids, seconds):
        mid[...] = ring.finish().astype(BF16)
        after.start()
    for ring in seconds:
        ring.forward()
    for ring, end in zip(seconds, ends):
        end[...] = ring.finish().astype(BF16)

    def last(f, end, land, rows, at_y, send):
        me = y if at_y else z
        for h in range(2):
            goal = 2 * j + h
            for i in range(2):
                here = jnp.logical_and(goal == me, i == j)
                device = dev(goal, z, x, i) if at_y else dev(y, goal, x, i)
                src = end.at[h, pl.ds(rows * i, rows)]
                n = 2 * h + i

                @pl.when(here)
                def _():
                    cp = pltpu.make_async_copy(src, land.at[me], lc.at[f])
                    if send == 0:
                        cp.start()
                    else:
                        cp.wait()

                @pl.when(jnp.logical_not(here))
                def _():
                    cp = remote(src, land.at[me], ls.at[f, n], lr.at[f, me], device)
                    if send == 0:
                        cp.start()
                    else:
                        cp.wait_send()

    def landed(f, end, land, rows, at_y, out):
        me = y if at_y else z
        mine = lax.div(me, 2) == j
        for m in range(4):
            here = jnp.logical_and(m == me, mine)

            @pl.when(jnp.logical_not(here))
            def _():
                remote(
                    end.at[0, pl.ds(0, rows)], land.at[m], ls.at[f, 0], lr.at[f, m], partner
                ).wait_recv()

        out[...] = (land[0].astype(F32) + land[1].astype(F32)) + (
            land[2].astype(F32) + land[3].astype(F32)
        )

    flows = (
        (0, q_end, q_land, 80, True, oq),
        (1, k_end, k_land, 80, True, okv),
        (2, o_end, o_land, 32, False, oo),
    )
    for f, end, land, rows, at_y, out in flows:
        last(f, end, land, rows, at_y, 0)
    for f, end, land, rows, at_y, out in flows:
        last(f, end, land, rows, at_y, 1)
    for flow in flows:
        landed(*flow)
    for ring in firsts + seconds:
        ring.drain()


def reduce_grads(gq, gkv, go):
    def buffers(half1, whole1, mid, half2, whole2, end, land):
        return [
            pltpu.VMEM((2,) + half1, BF16),
            pltpu.VMEM((2,) + whole1, BF16),
            pltpu.VMEM(mid, BF16),
            pltpu.VMEM((2,) + half2, BF16),
            pltpu.VMEM((2,) + whole2, BF16),
            pltpu.VMEM(end, BF16),
            pltpu.VMEM((4,) + land, BF16),
        ]

    wide = buffers(
        (4, 160, 256), (2, 4, 160, 256), (2, 4, 160, 256),
        (160, 256), (2, 160, 256), (2, 160, 256), (80, 256),
    )
    tall = buffers(
        (4, 64, 640), (2, 4, 64, 640), (2, 4, 64, 640),
        (64, 640), (2, 64, 640), (2, 64, 640), (32, 640),
    )
    return comm_call(
        reduce_kernel,
        "reduce_grads",
        3,
        (sds((80, 256), F32), sds((80, 256), F32), sds((32, 640), F32)),
        wide
        + wide
        + tall
        + [DMA((3, 2, 4)), DMA((3, 2, 4)), DMA((3, 4)), DMA((3, 4)), DMA((3,))],
        3,
    )(gq, gkv, go)


def per_device(
    tokens,
    doc_ids,
    cotangent,
    input_gain,
    query_weight,
    key_weight,
    value_weight,
    output_weight,
    query_gain,
    key_gain,
    post_gain,
):
    seq_count, shard_size, width = tokens.shape
    c = lax.axis_index("ctx")
    core = lax.rem(c, 2)
    tok = tokens.reshape(ROWS, D)
    cot = cotangent.reshape(ROWS, D)
    wide = tok.astype(F32)
    scale = lax.rsqrt(jnp.mean(wide * wide, axis=-1, keepdims=True) + EPS)
    normed = (wide * scale * input_gain).astype(BF16)
    line = jnp.pad(doc_ids.reshape(1, ROWS).astype(BF16), ((0, 0), (0, D - ROWS)))
    at = lax.broadcasted_iota(jnp.int32, (NOTE_ROWS, 1), 0)
    notes = jnp.where(at == 8 * core, line, jnp.zeros((), BF16))
    noted = jnp.concatenate([normed, notes], axis=0)

    start = lax.div(c, 2) * 256
    positions = (start + jnp.arange(256, dtype=jnp.int32)).astype(F32)
    exponents = jnp.arange(128, dtype=jnp.int32).astype(F32) * (2.0 / 256)
    angles = positions[:, None] * ROPE_BASE ** (-exponents)

    def table(values):
        values = values.reshape(2, 1, 128, 128)
        return jnp.broadcast_to(values, (2, 3, 128, 128)).reshape(2 * ROWS, 128)

    cos, sin = table(jnp.cos(angles)), table(jnp.sin(angles))
    gains = jnp.pad(jnp.stack([query_gain, key_gain]), ((0, 6), (0, 0)))
    base = start.reshape(1).astype(jnp.int32)

    n2, w = gather(noted, query_weight, key_weight, value_weight)
    q, unit, raw = project(n2, w, cos, sin, gains)
    halo, wo, wfull = exchange_halo(
        unit, output_weight.reshape(2, 128, D), w
    )
    attended, soft = attend_forward(q, unit, halo, base)
    attended = attended.reshape(2, ROWS, 512)
    (att,) = swap("swap_attended", 4, attended)
    layer_out, gp, ga = output_stage(
        att, wo.reshape(1024, D), tok, cot, post_gain.reshape(1, D)
    )
    grad, gp2 = swap("swap_grads", 5, ga, gp)
    qd, own, parts = attend_backward(q, unit, halo, soft, grad, raw, cos, sin, gains)
    total = return_grads(parts, own)
    go = out_grads(attended.reshape(2 * ROWS, 512), gp2)
    gq, gkv, kvd = in_grads(
        n2, total.reshape(2 * ROWS, 512), raw, cos, sin, gains, qd.reshape(2 * ROWS, 512)
    )
    (dq,) = swap("swap_query_deltas", 6, qd.reshape(2, ROWS, 512))
    (dkv,) = swap("swap_key_deltas", 7, kvd.reshape(2, ROWS, 512))
    tokens_grad = input_stage(dq, dkv, wfull, tok, cot, input_gain.reshape(1, D))
    oq, okv, oo = reduce_grads(gq, gkv, go)
    shape = (seq_count, shard_size, width)
    return (
        layer_out.reshape(shape),
        tokens_grad.reshape(shape),
        oq,
        okv[:, :128],
        okv[:, 128:],
        oo,
    )


def solution(mesh):
    placed = (
        P("fsdp", "ctx", None),
        P("fsdp", "ctx"),
        P("fsdp", "ctx", None),
        P(),
        P("fsdp", None),
        P("fsdp", None),
        P("fsdp", None),
        P("fsdp", None),
        P(),
        P(),
        P(),
    )
    return jax.shard_map(
        per_device,
        mesh=mesh,
        in_specs=placed,
        out_specs=(
            P("fsdp", "ctx", None),
            P("fsdp", "ctx", None),
            P("ctx", "fsdp"),
            P("ctx", "fsdp"),
            P("ctx", "fsdp"),
            P("ctx", "fsdp"),
        ),
        check_vma=False,
    )
```

```python
import functools

import jax
import jax.numpy as jnp
from jax import lax
from jax.experimental import pallas as pl
from jax.experimental.pallas import tpu as pltpu
from jax.sharding import PartitionSpec as P

EPS = 1e-06
ROPE_BASE = 10000.0
Q_FACTOR = 0.0625
WINDOW = 1024
F32 = jnp.float32
BF16 = jnp.bfloat16
MESH = pl.DeviceIdType.MESH
VMEM_LIMIT = 64 * 1024 * 1024 - 512 * 1024

D = 2560
ROWS = 384
NOTE_ROWS = 16
UNIT = 2 * ROWS + NOTE_ROWS


def place():
    y = lax.axis_index("fsdp")
    c = lax.axis_index("ctx")
    j = lax.rem(c, 2)
    zx = lax.div(c, 2)
    return y, lax.div(zx, 4), lax.rem(zx, 4), j


def dev(y, z, x, j):
    return (y, (z * 4 + x) * 2 + j)


def up(a, n=1):
    return lax.rem(a + n, 4)


def remote(src, dst, ss, rs, device):
    return pltpu.make_async_remote_copy(
        src_ref=src, dst_ref=dst, send_sem=ss, recv_sem=rs, device_id=device, device_id_type=MESH
    )


def meet(devices):
    barrier = pltpu.get_barrier_semaphore()
    for device in devices:
        pl.semaphore_signal(barrier, inc=1, device_id=device, device_id_type=MESH)
    pl.semaphore_wait(barrier, len(devices))


def rows_at(start, size, unit=16):
    return pl.ds(pl.multiple_of(start, unit), size)


def vmem(n):
    return [pl.BlockSpec(memory_space=pltpu.VMEM)] * n


def spaces(kinds):
    where = {"v": pltpu.VMEM, "h": pl.ANY}
    return [pl.BlockSpec(memory_space=where[kind]) for kind in kinds]


def comm_call(kernel, name, cid, out_shape, scratch, ins, outs):
    return pl.pallas_call(
        kernel,
        name=name,
        out_shape=list(out_shape),
        in_specs=spaces(ins),
        out_specs=spaces(outs),
        scratch_shapes=scratch,
        compiler_params=pltpu.CompilerParams(
            collective_id=cid, has_side_effects=True, vmem_limit_bytes=VMEM_LIMIT
        ),
    )


def sds(shape, dtype):
    return jax.ShapeDtypeStruct(shape, dtype)


DMA = pltpu.SemaphoreType.DMA


class RingGather:
    def __init__(self, me, plus, minus, region, half, ss, rs, index):
        self.me, self.plus, self.minus = me, plus, minus
        self.region, self.half, self.ss, self.rs, self.index = region, half, ss, rs, index

    def _copy(self, ref, k, device):
        at = self.index + (k,)
        return remote(ref, ref, self.ss.at[at], self.rs.at[at], device)

    def start(self):
        self._copy(self.region(self.me), 0, self.plus).start()
        self._copy(self.region(self.me), 1, self.minus).start()

    def forward(self):
        left, right = up(self.me, 3), up(self.me, 1)
        self._copy(self.region(left), 0, self.plus).wait_recv()
        self._copy(self.half(left, 0), 2, self.plus).start()
        self._copy(self.region(right), 1, self.minus).wait_recv()
        self._copy(self.half(right, 1), 3, self.minus).start()

    def finish(self):
        far = up(self.me, 2)
        self._copy(self.half(far, 0), 2, self.plus).wait_recv()
        self._copy(self.half(far, 1), 3, self.minus).wait_recv()

    def drain(self):
        self._copy(self.region(self.me), 0, self.plus).wait_send()
        self._copy(self.region(self.me), 1, self.minus).wait_send()
        self._copy(self.half(up(self.me, 3), 0), 2, self.plus).wait_send()
        self._copy(self.half(up(self.me, 1), 1), 3, self.minus).wait_send()


PLANE = 96


def gather_kernel(n_ref, wq, wk, wv, n2, w, lsem, nsem, ysend, yrecv, gsend, grecv, rsend, rrecv):
    y, z, x, j = place()
    partner = dev(y, z, x, 1 - j)
    xp, xm = dev(y, z, up(x), j), dev(y, z, up(x, 3), j)
    zp, zm = dev(y, up(z), x, j), dev(y, up(z, 3), x, j)
    ys = [dev(up(y, r), z, x, j) for r in (1, 2, 3)]
    own = rows_at(640 * y, 640)
    local = []
    for b in range(8):
        if b < 4:
            src = wq.at[:, pl.ds(pl.multiple_of(512 * j + 128 * b, 128), 128)]
        elif b < 6:
            src = wk.at[:, pl.ds(pl.multiple_of(256 * j + 128 * (b - 4), 128), 128)]
        else:
            src = wv.at[:, pl.ds(pl.multiple_of(256 * j + 128 * (b - 6), 128), 128)]
        local.append(pltpu.make_async_copy(src, w.at[b, own], lsem.at[b]))
    local.append(pltpu.make_async_copy(n_ref, n2.at[j], lsem.at[8]))
    for cp in local:
        cp.start()
    meet([partner, xp, xm, zp, zm] + ys)
    for cp in local[:8]:
        cp.wait()

    def piece_q(yy):
        return w.at[x, rows_at(640 * yy + PLANE * z, PLANE)]

    def piece_k(yy):
        return w.at[4 + z, rows_at(640 * yy + PLANE * x, PLANE)]

    straight = RingGather(
        y,
        ys[0],
        ys[2],
        lambda m: w.at[:, rows_at(640 * m + 4 * PLANE, 640 - 4 * PLANE)],
        lambda m, h: w.at[pl.ds(4 * h, 4), rows_at(640 * m + 4 * PLANE, 640 - 4 * PLANE)],
        rsend,
        rrecv,
        (),
    )

    first = []
    for r in range(3):
        for f, piece in enumerate((piece_q, piece_k)):
            cp = remote(piece(y), piece(y), ysend.at[f, r], yrecv.at[f, r], ys[r])
            cp.start()
            first.append((cp, f, r, piece))
    straight.start()
    swap = remote(n_ref, n2.at[j], nsem.at[0], nsem.at[1], partner)
    swap.start()

    def ring(f, stage, r):
        yy = up(y, 3 - r)
        first, count = 4 * f, PLANE // 2
        if stage == 0:
            inner = z if f == 0 else x
            region = lambda m: w.at[first + m, rows_at(640 * yy + PLANE * inner, PLANE)]
            half = lambda m, h: w.at[
                first + m, rows_at(640 * yy + PLANE * inner + count * h, count)
            ]
        else:
            region = lambda m: w.at[pl.ds(first, 4), rows_at(640 * yy + PLANE * m, PLANE)]
            half = lambda m, h: w.at[
                pl.ds(first + 2 * h, 2), rows_at(640 * yy + PLANE * m, PLANE)
            ]
        on_x = (f + stage) % 2 == 0
        me, plus, minus = (x, xp, xm) if on_x else (z, zp, zm)
        return RingGather(me, plus, minus, region, half, gsend, grecv, (f, stage, r))

    rings = [[[ring(f, s, r) for r in range(3)] for s in range(2)] for f in range(2)]
    for cp, f, r, piece in first:
        yy = up(y, 3 - r)
        remote(piece(yy), piece(yy), ysend.at[f, r], yrecv.at[f, r], ys[r]).wait_recv()
        rings[f][0][r].start()
    for r in range(3):
        for f in range(2):
            rings[f][0][r].forward()
    for r in range(3):
        for f in range(2):
            rings[f][0][r].finish()
            rings[f][1][r].start()
    straight.forward()
    for r in range(3):
        for f in range(2):
            rings[f][1][r].forward()
    for r in range(3):
        for f in range(2):
            rings[f][1][r].finish()
    for r in range(3):
        for f in range(2):
            rings[f][0][r].drain()
            rings[f][1][r].drain()
    straight.finish()
    straight.drain()
    for cp, f, r, piece in first:
        cp.wait_send()
    swap.wait()
    local[8].wait()


def gather(noted, wq, wk, wv):
    return comm_call(
        gather_kernel,
        "gather_weights",
        0,
        (sds((2, ROWS + NOTE_ROWS, D), BF16), sds((8, D, 128), BF16)),
        [
            DMA((9,)),
            DMA((2,)),
            DMA((2, 3)),
            DMA((2, 3)),
            DMA((2, 2, 3, 4)),
            DMA((2, 2, 3, 4)),
            DMA((4,)),
            DMA((4,)),
        ],
        "vvvv",
        "hh",
    )(noted, wq, wk, wv)


def project_kernel(n2, w, cos, sin, gains, q_out, unit, raw_out):
    n = pl.program_id(0)
    rows = n2[:, :ROWS, :].reshape(2 * ROWS, D)
    weight = jnp.concatenate([w[0], w[1]], axis=-1)
    acc = jnp.dot(rows, weight, preferred_element_type=F32)

    def rotated(gain, factor):
        scale = lax.rsqrt(jnp.mean(acc * acc, axis=-1, keepdims=True) + EPS)
        normed = acc * scale * gain
        a, b = normed[:, :128], normed[:, 128:]
        c, s = cos[...], sin[...]
        return (jnp.concatenate([a * c - b * s, b * c + a * s], axis=-1) * factor).astype(BF16)

    @pl.when(n < 3)
    def _():
        raw_out[0] = acc

    @pl.when(n < 2)
    def _():
        q_out[0] = rotated(gains[0:1, :], Q_FACTOR)

    @pl.when(n == 2)
    def _():
        unit[0 : 2 * ROWS, 0:256] = rotated(gains[1:2, :], 1.0)

    @pl.when(n == 3)
    def _():
        unit[0 : 2 * ROWS, 256:512] = acc.astype(BF16)
        unit[2 * ROWS : UNIT, :] = n2[0, ROWS:, 0:512] + n2[1, ROWS:, 0:512]


def project(n2, w, cos, sin, gains):
    return pl.pallas_call(
        project_kernel,
        name="project",
        grid=(4,),
        in_specs=[
            pl.BlockSpec((2, ROWS + NOTE_ROWS, D), lambda n: (0, 0, 0)),
            pl.BlockSpec((2, D, 128), lambda n: (n, 0, 0)),
            pl.BlockSpec((2 * ROWS, 128), lambda n: (0, 0)),
            pl.BlockSpec((2 * ROWS, 128), lambda n: (0, 0)),
            pl.BlockSpec((8, 256), lambda n: (0, 0)),
        ],
        out_specs=[
            pl.BlockSpec((1, 2 * ROWS, 256), lambda n: (jnp.minimum(n, 1), 0, 0)),
            pl.BlockSpec((UNIT, 512), lambda n: (0, 0)),
            pl.BlockSpec((1, 2 * ROWS, 256), lambda n: (jnp.minimum(n, 2), 0, 0)),
        ],
        out_shape=[
            sds((2, 2 * ROWS, 256), BF16),
            sds((UNIT, 512), BF16),
            sds((3, 2 * ROWS, 256), F32),
        ],
        compiler_params=pltpu.CompilerParams(vmem_limit_bytes=VMEM_LIMIT),
    )(n2, w, cos, sin, gains)


HALO_CHUNKS = 7
HALO_ROWS = UNIT // HALO_CHUNKS


def halo_kernel(unit, wo_own, w, halo, wo, wother, hsend, hrecv, osend, orecv, lsem, wsem):
    y, z, x, j = place()
    partner = dev(y, z, x, 1 - j)
    xp, xm = dev(y, z, up(x), j), dev(y, z, up(x, 3), j)
    zp, zm = dev(y, up(z), x, j), dev(y, up(z, 3), x, j)
    yp, ym = dev(up(y), z, x, j), dev(up(y, 3), z, x, j)
    ocopy = pltpu.make_async_copy(wo_own, wo.at[y], lsem.at[1])
    ocopy.start()
    meet([partner, xp, xm, zp, zm, yp, ym])

    def rows(k):
        return rows_at(k * HALO_ROWS, HALO_ROWS)

    def shift(k):
        return remote(unit.at[rows(k)], halo.at[3, rows(k)], hsend.at[0, k], hrecv.at[0, k], zp)

    def right(src, k):
        return remote(src.at[rows(k)], halo.at[0, rows(k)], hsend.at[1, k], hrecv.at[1, k], xp)

    def left(src, k):
        return remote(src.at[rows(k)], halo.at[2, rows(k)], hsend.at[2, k], hrecv.at[2, k], xm)

    def far_right(k):
        return remote(
            halo.at[0, rows(k)], halo.at[1, rows(k)], hsend.at[3, k], hrecv.at[3, k], xp
        )

    def far_left(k):
        return remote(
            halo.at[2, rows(k)], halo.at[1, rows(k)], hsend.at[4, k], hrecv.at[3, k], xm
        )

    before = halo.at[3]
    inner = jnp.logical_and(x > 0, x < 3)

    @pl.loop(0, HALO_CHUNKS)
    def _(k):
        shift(k).start()

        @pl.when(x < 3)
        def _():
            right(unit, k).start()

        @pl.when(x == 0)
        def _():
            left(unit, k).start()

    ocopy.wait()
    ring = RingGather(
        y,
        yp,
        ym,
        lambda m: wo.at[m, j],
        lambda m, h: wo.at[m, j, pl.ds(64 * h, 64)],
        osend,
        orecv,
        (0,),
    )
    ring.start()
    swap = remote(w, wother, wsem.at[0], wsem.at[1], partner)
    swap.start()

    def step(k):
        shift(k).wait_recv()

        @pl.when(x == 3)
        def _():
            right(before, k).start()

        @pl.when(x > 0)
        def _():
            left(before, k).start()

        right(unit, k).wait_recv()

        @pl.when(inner)
        def _():
            far_right(k).start()

        @pl.when(k > 0)
        def _():
            left(unit, k - 1).wait_recv()

            @pl.when(inner)
            def _():
                far_left(k - 1).start()

    pl.loop(0, 4)(step)
    ring.forward()
    share = []

    def give(n, m):
        cp = remote(wo.at[m, j], wo.at[m, j], osend.at[1, n], orecv.at[1, n], partner)
        cp.start()
        share.append(cp)

    give(0, up(y, 3))
    give(1, up(y, 1))
    pl.loop(4, HALO_CHUNKS)(step)
    left(unit, HALO_CHUNKS - 1).wait_recv()

    @pl.when(inner)
    def _():
        far_left(HALO_CHUNKS - 1).start()

    ring.finish()
    give(2, up(y, 2))
    for n, m in enumerate((up(y, 3), up(y, 1), up(y, 2))):
        remote(
            wo.at[m, 1 - j], wo.at[m, 1 - j], osend.at[1, n], orecv.at[1, n], partner
        ).wait_recv()
    for cp in share:
        cp.wait_send()
    ring.drain()

    @pl.loop(0, HALO_CHUNKS)
    def _(k):
        far_right(k).wait_recv()
        shift(k).wait_send()
        right(unit, k).wait_send()
        left(unit, k).wait_send()

        @pl.when(inner)
        def _():
            far_right(k).wait_send()
            far_left(k).wait_send()

    swap.wait()


def exchange_halo(unit, wo_own, w):
    return comm_call(
        halo_kernel,
        "exchange_halo",
        1,
        (
            sds((4, UNIT, 512), BF16),
            sds((4, 2, 128, D), BF16),
            sds((8, D, 128), BF16),
        ),
        [
            DMA((5, HALO_CHUNKS)),
            DMA((4, HALO_CHUNKS)),
            DMA((2, 4)),
            DMA((2, 4)),
            DMA((2,)),
            DMA((2,)),
        ],
        "vvh",
        "hhh",
    )(unit, wo_own, w)


KEYS = 1280


def window_of(unit, halo, s, first, last):
    parts = []
    for d in (4, 3, 2, 1, 0):
        for i in range(2):
            at = rows_at(i * ROWS + s * 128, 128)
            if d == 0:
                parts.append(unit[at, first:last])
            else:
                parts.append(halo[d - 1, at, first:last])
    return jnp.concatenate(parts, axis=0)


def map_back(upstream, raw, c, s, gain, factor):
    a, b = upstream[:, :128] * factor, upstream[:, 128:] * factor
    turned = jnp.concatenate([a * c + b * s, b * c - a * s], axis=-1) * gain
    scale = lax.rsqrt(jnp.mean(raw * raw, axis=-1, keepdims=True) + EPS)
    inner = jnp.mean(turned * raw, axis=-1, keepdims=True)
    return scale * turned - raw * (scale * scale * scale * inner)


def add_into(ref, at, other):
    ref[at] = (ref[at].astype(F32) + other.astype(F32)).astype(BF16)


class RingReduce:
    def __init__(self, me, plus, minus, data, pick, half, relay, recv, ss, rs, index):
        self.me, self.plus, self.minus = me, plus, minus
        self.data, self.pick, self.half = data, pick, half
        self.relay, self.recv, self.ss, self.rs, self.index = relay, recv, ss, rs, index

    def _copy(self, src, dst, k, device):
        at = self.index + (k,)
        return remote(src, dst, self.ss.at[at], self.rs.at[at], device)

    def _first(self):
        far = up(self.me, 2)
        return (
            self._copy(self.data.at[self.half(far, 0)], self.relay.at[0], 0, self.plus),
            self._copy(self.data.at[self.half(far, 1)], self.relay.at[1], 1, self.minus),
        )

    def _second(self):
        right, left = up(self.me, 1), up(self.me, 3)
        return (
            self._copy(self.data.at[self.pick(right)], self.recv.at[0], 2, self.plus),
            self._copy(self.data.at[self.pick(left)], self.recv.at[1], 3, self.minus),
        )

    def start(self):
        for cp in self._first():
            cp.start()

    def forward(self):
        a, b = self._first()
        c, d = self._second()
        a.wait_recv()
        add_into(self.data, self.half(up(self.me, 1), 0), self.relay[0])
        c.start()
        b.wait_recv()
        add_into(self.data, self.half(up(self.me, 3), 1), self.relay[1])
        d.start()

    def finish(self):
        c, d = self._second()
        c.wait_recv()
        d.wait_recv()
        return (
            self.data[self.pick(self.me)].astype(F32)
            + self.recv[0].astype(F32)
            + self.recv[1].astype(F32)
        )

    def drain(self):
        for cp in self._first() + self._second():
            cp.wait_send()


def middle_kernel(
    q, unit, halo, base, wo_h, tok_h, cot_h, gain, raw_h, cos, sin, gains, n2_h,
    layer_out, own, parts, qd, o_mid, gq,
    wo, tok, cot, raw, n2, soft, att, attx, proj, gp2, grad, grad_send, go, o_relay, o_recv,
    loadsem, asend, arecv, gsend, grecv, dsem, ss, rs,
):
    y, z, x, j = place()
    partner = dev(y, z, x, 1 - j)
    yp, ym = dev(up(y), z, x, j), dev(up(y, 3), z, x, j)
    loads = [
        pltpu.make_async_copy(src, dst, loadsem.at[n])
        for n, (src, dst) in enumerate(
            ((wo_h, wo), (tok_h, tok), (cot_h, cot), (raw_h.at[pl.ds(0, 2)], raw), (n2_h, n2))
        )
    ]
    for cp in loads:
        cp.start()
    meet([partner, yp, ym])

    def give_attended(s):
        return remote(att.at[1 - j, s], attx.at[s], asend.at[s], arecv.at[s], partner)

    key_at = lax.broadcasted_iota(jnp.int32, (256, KEYS), 1) - WINDOW
    query_at = lax.broadcasted_iota(jnp.int32, (256, KEYS), 0)

    @pl.loop(0, 3)
    def _(s):
        keys = window_of(unit, halo, s, 0, 256)
        values = window_of(unit, halo, s, 256, 512)
        lanes = pl.ds(pl.multiple_of(s * 128, 128), 128)
        notes = []
        for d in (4, 3, 2, 1, 0):
            block = unit[2 * ROWS :, lanes] if d == 0 else halo[d - 1, 2 * ROWS :, lanes]
            block = block.astype(F32)
            notes.extend([block[0:1], block[8:9]])
        key_docs = jnp.concatenate(notes, axis=-1)
        query_docs = jnp.concatenate(
            [jnp.transpose(jnp.broadcast_to(note, (128, 128))) for note in notes[8:]], axis=0
        )
        query_docs = jnp.concatenate([query_docs] * (KEYS // 128), axis=-1)
        allowed = (
            (query_docs == key_docs)
            & (key_at <= query_at)
            & (key_at > query_at - WINDOW)
            & (key_at + base[0:1, 0:1] >= 0)
        )
        for h in range(2):
            rows = q[h, :, s].reshape(256, 256)
            scores = lax.dot_general(
                rows, keys, (((1,), (1,)), ((), ())), preferred_element_type=F32
            )
            masked = jnp.where(allowed, scores, -1e30)
            highest = jnp.max(masked, axis=-1, keepdims=True)
            raised = jnp.exp(masked - highest)
            weights = (raised / jnp.sum(raised, axis=-1, keepdims=True)).astype(BF16)
            soft[s, 256 * h : 256 * h + 256, :] = weights
            out = jnp.dot(weights, values, preferred_element_type=F32).astype(BF16)
            att[:, s, :, 256 * h : 256 * h + 256] = out.reshape(2, 128, 256)
        give_attended(s).start()

    for cp in loads[:3]:
        cp.wait()
    for s in range(3):
        give_attended(s).wait_recv()
    mine, others = att[j].reshape(ROWS, 512), attx[...].reshape(ROWS, 512)
    own_heads, other_heads = rows_at(512 * j, 512), rows_at(512 * (1 - j), 512)

    @pl.loop(0, 5)
    def _(n):
        cols = pl.ds(pl.multiple_of(512 * n, 512), 512)
        proj[:, cols] = jnp.dot(
            mine, wo[own_heads, cols], preferred_element_type=F32
        ) + jnp.dot(others, wo[other_heads, cols], preferred_element_type=F32)

    def give_projected(t):
        at = pl.ds(128 * t, 128)
        return remote(gp2.at[0, at], gp2.at[1, at], gsend.at[t], grecv.at[t], partner)

    for t in range(3):

        @pl.loop(8 * t, 8 * t + 8)
        def _(k):
            at = rows_at(k * 16, 16)
            p = proj[at, :]
            g = gain[...]
            scale = lax.rsqrt(jnp.mean(p * p, axis=-1, keepdims=True) + EPS)
            layer_out[at, :] = (tok[at, :].astype(F32) + p * scale * g).astype(BF16)
            h = cot[at, :].astype(F32) * g
            inner = jnp.mean(h * p, axis=-1, keepdims=True)
            gp2[0, at, :] = (scale * h - p * (scale * scale * scale * inner)).astype(BF16)

        give_projected(t).start()

    upstream = gp2[0]

    def attended_grad(heads):
        part = lax.dot_general(
            upstream, wo[heads, :], (((1,), (1,)), ((), ())), preferred_element_type=F32
        )
        return part.astype(BF16).reshape(3, 128, 512)

    grad_send[...] = attended_grad(other_heads)
    give_grad = remote(grad_send, grad.at[j], dsem.at[0], dsem.at[1], partner)
    give_grad.start()
    grad[j] = attended_grad(own_heads)
    for t in range(3):
        give_projected(t).wait_recv()
    across = (((0,), (0,)), ((), ()))
    other_rows = att[1 - j].reshape(ROWS, 512)
    for n in range(4):
        cols = slice(640 * n, 640 * n + 640)
        term = lax.dot_general(
            mine, gp2[0, :, cols], across, preferred_element_type=F32
        ) + lax.dot_general(other_rows, gp2[1, :, cols], across, preferred_element_type=F32)
        go[n] = term.astype(BF16).reshape(2, 4, 64, 640)
    o1 = RingReduce(
        y, yp, ym, go, lambda m: (m,), lambda m, h: (m, h), o_relay, o_recv, ss, rs, ()
    )
    o1.start()
    loads[3].wait()
    give_grad.wait_recv()

    def backward(first, last):
        @pl.loop(first, last)
        def _(s):
            keys = window_of(unit, halo, s, 0, 256)
            values = window_of(unit, halo, s, 256, 512)
            grads = jnp.concatenate(
                [grad[:, s, :, 256 * h : 256 * h + 256].reshape(256, 256) for h in range(2)],
                axis=0,
            )
            weights = soft[s]

            def emit(part, first_col):
                for n, d in enumerate((4, 3, 2, 1, 0)):
                    for i in range(2):
                        piece = part[256 * n + 128 * i : 256 * n + 128 * i + 128]
                        if d == 0:
                            own[i, s, :, first_col : first_col + 256] = piece
                        else:
                            parts[d - 1, i, s, :, first_col : first_col + 256] = piece.astype(BF16)

            emit(lax.dot_general(weights, grads, across, preferred_element_type=F32), 256)
            grad_weights = lax.dot_general(
                grads, values, (((1,), (1,)), ((), ())), preferred_element_type=F32
            )
            wide = weights.astype(F32)
            moved = wide * grad_weights
            dots = jnp.sum(moved, axis=-1, keepdims=True)
            score_grads = (moved - wide * dots).astype(BF16)
            grad_queries = jnp.dot(score_grads, keys, preferred_element_type=F32)
            queries = jnp.concatenate(
                [q[h, :, s].reshape(256, 256) for h in range(2)], axis=0
            )
            emit(lax.dot_general(score_grads, queries, across, preferred_element_type=F32), 0)
            c, sn = cos[:, s].reshape(256, 128), sin[:, s].reshape(256, 128)
            for h in range(2):
                back = map_back(
                    grad_queries[256 * h : 256 * h + 256],
                    raw[h, :, s].reshape(256, 256),
                    c,
                    sn,
                    gains[0:1, :],
                    Q_FACTOR,
                )
                qd[:, s, :, 256 * h : 256 * h + 256] = back.astype(BF16).reshape(2, 128, 256)

    backward(0, 2)
    o1.forward()
    backward(2, 3)
    loads[4].wait()

    @pl.loop(0, 4)
    def _(n):
        rows = n2[:, :ROWS, pl.ds(pl.multiple_of(640 * n, 128), 640)].reshape(2 * ROWS, 640)
        for h in range(2):
            deltas = qd[:, :, :, 256 * h : 256 * h + 256].reshape(2 * ROWS, 256)
            term = lax.dot_general(rows, deltas, across, preferred_element_type=F32)
            gq[h, n] = term.astype(BF16).reshape(4, 160, 256)

    o_mid[...] = o1.finish().astype(BF16)
    o1.drain()
    for s in range(3):
        give_attended(s).wait_send()
        give_projected(s).wait_send()
    give_grad.wait_send()


def middle(q, unit, halo, base, wo, tok, cot, gain, raw, cos, sin, gains, n2):
    return comm_call(
        middle_kernel,
        "middle",
        4,
        (
            sds((ROWS, D), BF16),
            sds((2, 3, 128, 512), F32),
            sds((4, 2, 3, 128, 512), BF16),
            sds((2, 3, 128, 512), BF16),
            sds((2, 4, 64, 640), BF16),
            sds((2, 4, 4, 160, 256), BF16),
        ),
        [
            pltpu.VMEM((1024, D), BF16),
            pltpu.VMEM((ROWS, D), BF16),
            pltpu.VMEM((ROWS, D), BF16),
            pltpu.VMEM((2, 2, 3, 128, 256), F32),
            pltpu.VMEM((2, ROWS + NOTE_ROWS, D), BF16),
            pltpu.VMEM((3, 512, KEYS), BF16),
            pltpu.VMEM((2, 3, 128, 512), BF16),
            pltpu.VMEM((3, 128, 512), BF16),
            pltpu.VMEM((ROWS, D), F32),
            pltpu.VMEM((2, ROWS, D), BF16),
            pltpu.VMEM((2, 3, 128, 512), BF16),
            pltpu.VMEM((3, 128, 512), BF16),
            pltpu.VMEM((4, 2, 4, 64, 640), BF16),
            pltpu.VMEM((2, 4, 64, 640), BF16),
            pltpu.VMEM((2, 2, 4, 64, 640), BF16),
            DMA((5,)),
            DMA((3,)),
            DMA((3,)),
            DMA((3,)),
            DMA((3,)),
            DMA((2,)),
            DMA((4,)),
            DMA((4,)),
        ],
        "vvvvhhhvhvvvh",
        "vvvvvv",
    )(
        q.reshape(2, 2, 3, 128, 256),
        unit,
        halo,
        base,
        wo,
        tok,
        cot,
        gain,
        raw.reshape(3, 2, 3, 128, 256),
        cos.reshape(2, 3, 128, 128),
        sin.reshape(2, 3, 128, 128),
        gains,
        n2,
    )


def key_grads_kernel(n2, total, raw, cos, sin, gains, gkv, kvd):
    @pl.when(pl.program_id(0) == 0)
    def _():
        kd = map_back(total[:, :256], raw[0], cos[...], sin[...], gains[1:2, :], 1.0)
        kvd[:, :256] = kd.astype(BF16)
        kvd[:, 256:] = total[:, 256:].astype(BF16)

    rows = n2[:, :ROWS, :].reshape(2 * ROWS, 640)
    for half in range(2):
        rhs = jnp.concatenate(
            [kvd[:, 128 * half : 128 * half + 128], kvd[:, 256 + 128 * half : 384 + 128 * half]],
            axis=-1,
        )
        term = lax.dot_general(rows, rhs, (((0,), (0,)), ((), ())), preferred_element_type=F32)
        term = term.astype(BF16).reshape(4, 2, 80, 256)
        for i in range(2):
            gkv[i, half, 0] = term[:, i]


def key_grads(n2, total, raw, cos, sin, gains):
    return pl.pallas_call(
        key_grads_kernel,
        name="key_grads",
        grid=(4,),
        in_specs=[
            pl.BlockSpec((2, ROWS + NOTE_ROWS, 640), lambda n: (0, 0, n)),
            pl.BlockSpec((2 * ROWS, 512), lambda n: (0, 0)),
            pl.BlockSpec((1, 2 * ROWS, 256), lambda n: (2, 0, 0)),
            pl.BlockSpec((2 * ROWS, 128), lambda n: (0, 0)),
            pl.BlockSpec((2 * ROWS, 128), lambda n: (0, 0)),
            pl.BlockSpec((8, 256), lambda n: (0, 0)),
        ],
        out_specs=[
            pl.BlockSpec((2, 2, 1, 4, 80, 256), lambda n: (0, 0, n, 0, 0, 0)),
            pl.BlockSpec((2 * ROWS, 512), lambda n: (0, 0)),
        ],
        out_shape=[
            sds((2, 2, 4, 4, 80, 256), BF16),
            sds((2 * ROWS, 512), BF16),
        ],
        compiler_params=pltpu.CompilerParams(vmem_limit_bytes=VMEM_LIMIT),
    )(n2, total, raw, cos, sin, gains)


CHUNKS = 6
EVERY = slice(None)


def send_last(end, land, sends, ls, lr, lc, start):
    for n, (src, slot, device, here) in enumerate(sends):

        @pl.when(here)
        def _():
            cp = pltpu.make_async_copy(src, land.at[slot], lc)
            if start:
                cp.start()
            else:
                cp.wait()

        @pl.when(jnp.logical_not(here))
        def _():
            cp = remote(src, land.at[slot], ls.at[n], lr.at[slot], device)
            if start:
                cp.start()
            else:
                cp.wait_send()


def sum_last(like, land, ls, lr, me, mine, partner, out):
    for m in range(4):

        @pl.when(jnp.logical_not(jnp.logical_and(m == me, mine)))
        def _():
            remote(like, land.at[m], ls.at[0], lr.at[m], partner).wait_recv()

    out[...] = (land[0].astype(F32) + land[1].astype(F32)) + (
        land[2].astype(F32) + land[3].astype(F32)
    )


def return_kernel(
    parts, own, o_mid, gq, qd,
    total, oo, q_mid, dq,
    relay, near, after, relayed, summed, bsum,
    o_relay2, o_recv2, o_end, o_land, q_relay, q_recv,
    ssem, rsem, ss, rs, ls, lr, lc, dsem,
):
    y, z, x, j = place()
    partner = dev(y, z, x, 1 - j)
    xp, xm = dev(y, z, up(x), j), dev(y, z, up(x, 3), j)
    zp, zm = dev(y, up(z), x, j), dev(y, up(z, 3), x, j)
    zfar = [dev(y, up(z, r), x, i) for r in (1, 2, 3) for i in (0, 1)]
    keep = pltpu.make_async_copy(qd.at[j], dq.at[0], dsem.at[0])
    keep.start()
    meet([partner, xp, xm] + zfar)
    inner = jnp.logical_and(x > 0, x < 3)
    low = x < 2

    def relay_left(k):
        return remote(parts.at[1, k], relay.at[0, k], ssem.at[0, k], rsem.at[0, k], xm)

    def relay_right(k):
        return remote(parts.at[1, k], relay.at[1, k], ssem.at[1, k], rsem.at[1, k], xp)

    def to_left(src, k):
        return remote(src.at[k], near.at[0, k], ssem.at[2, k], rsem.at[2, k], xm)

    def to_right(src, k):
        return remote(src.at[k], near.at[1, k], ssem.at[3, k], rsem.at[3, k], xp)

    def back(k):
        return remote(bsum.at[k], after.at[k], ssem.at[4, k], rsem.at[4, k], zm)

    q1 = RingReduce(
        z, zp, zm, gq, lambda m: (EVERY, m), lambda m, h: (h, m), q_relay, q_recv, ss, rs, (0,)
    )
    o2 = RingReduce(
        x, xp, xm, o_mid, lambda m: (EVERY, m), lambda m, h: (h, m),
        o_relay2, o_recv2, ss, rs, (1,),
    )

    q1.start()
    o2.start()

    @pl.loop(0, CHUNKS)
    def _(k):
        @pl.when(low)
        def _():
            relay_right(k).start()

        @pl.when(jnp.logical_not(low))
        def _():
            relay_left(k).start()

        @pl.when(jnp.logical_not(inner))
        def _():
            to_left(parts.at[0], k).start()
            to_right(parts.at[2], k).start()

    give = remote(qd.at[1 - j], dq.at[1], dsem.at[1], dsem.at[2], partner)
    give.start()

    def relay_step(first, last):
        @pl.when(inner)
        def _():
            @pl.loop(first, last)
            def _(k):
                relay_left(k).wait_recv()
                relayed[0, k] = (parts[0, k].astype(F32) + relay[0, k].astype(F32)).astype(BF16)
                to_left(relayed.at[0], k).start()
                relay_right(k).wait_recv()
                relayed[1, k] = (parts[2, k].astype(F32) + relay[1, k].astype(F32)).astype(BF16)
                to_right(relayed.at[1], k).start()

    def near_step(first, last):
        @pl.loop(first, last)
        def _(k):
            to_left(parts.at[0], k).wait_recv()
            to_right(parts.at[2], k).wait_recv()
            from_right = near[0, k].astype(F32)
            from_left = near[1, k].astype(F32)
            zero = jnp.zeros_like(from_left)
            near_a = jnp.where(x < 3, from_right, zero) + jnp.where(x == 0, from_left, zero)
            near_b = jnp.where(x == 3, from_right, zero) + jnp.where(x > 0, from_left, zero)
            summed[k] = near_a
            bsum[k] = (parts[3, k].astype(F32) + near_b).astype(BF16)
            back(k).start()

    relay_step(0, 2)
    q1.forward()
    relay_step(2, 4)
    o2.forward()
    relay_step(4, CHUNKS)
    near_step(0, 3)
    q_mid[...] = q1.finish().astype(BF16)
    near_step(3, CHUNKS)

    o_end[...] = o2.finish().astype(BF16)
    o_sends = []
    for h in range(2):
        for i in range(2):
            goal = 2 * j + h
            o_sends.append(
                (
                    o_end.at[h, pl.ds(32 * i, 32)],
                    z,
                    dev(y, goal, x, i),
                    jnp.logical_and(goal == z, i == j),
                )
            )
    send_last(o_end, o_land, o_sends, ls, lr, lc, True)

    @pl.loop(0, CHUNKS)
    def _(k):
        back(k).wait_recv()
        total[k] = own[k] + summed[k] + after[k].astype(F32)

    send_last(o_end, o_land, o_sends, ls, lr, lc, False)
    sum_last(o_end.at[0, pl.ds(0, 32)], o_land, ls, lr, z, lax.div(z, 2) == j, partner, oo)

    @pl.loop(0, CHUNKS)
    def _(k):
        @pl.when(low)
        def _():
            relay_right(k).wait_send()

        @pl.when(jnp.logical_not(low))
        def _():
            relay_left(k).wait_send()

        to_left(parts.at[0], k).wait_send()
        to_right(parts.at[2], k).wait_send()
        back(k).wait_send()

    for ring in (q1, o2):
        ring.drain()
    keep.wait()
    give.wait()


def return_grads(parts, own, o_mid, gq, qd):
    block = (CHUNKS, 128, 512)
    return comm_call(
        return_kernel,
        "return_grads",
        2,
        (
            sds(block, F32),
            sds((32, 640), F32),
            sds((2, 4, 160, 256), BF16),
            sds((2, ROWS, 512), BF16),
        ),
        [
            pltpu.VMEM((2,) + block, BF16),
            pltpu.VMEM((2,) + block, BF16),
            pltpu.VMEM(block, BF16),
            pltpu.VMEM((2,) + block, BF16),
            pltpu.VMEM(block, F32),
            pltpu.VMEM(block, BF16),
            pltpu.VMEM((2, 64, 640), BF16),
            pltpu.VMEM((2, 2, 64, 640), BF16),
            pltpu.VMEM((2, 64, 640), BF16),
            pltpu.VMEM((4, 32, 640), BF16),
            pltpu.VMEM((2, 4, 160, 256), BF16),
            pltpu.VMEM((2, 2, 4, 160, 256), BF16),
            DMA((5, CHUNKS)),
            DMA((5, CHUNKS)),
            DMA((2, 4)),
            DMA((2, 4)),
            DMA((4,)),
            DMA((4,)),
            DMA(()),
            DMA((3,)),
        ],
        "vvvvv",
        "vvvv",
    )(parts.reshape((4,) + block), own.reshape(block), o_mid, gq, qd)


def finish_kernel(
    gkv, kvd, dq, q_mid, w, wother, tok, cot, gain,
    okv, oq, out,
    dkv, w_buf, tok_buf, cot_buf, acc,
    relay, recv, mid, relay2, recv2, end, land, q_relay, q_recv, q_end, q_land,
    ss, rs, ls, lr, lc, dsem, msem,
):
    y, z, x, j = place()
    partner = dev(y, z, x, 1 - j)
    xp, xm = dev(y, z, up(x), j), dev(y, z, up(x, 3), j)
    zp, zm = dev(y, up(z), x, j), dev(y, up(z, 3), x, j)
    yfar = [dev(up(y, r), z, x, i) for r in (1, 2, 3) for i in (0, 1)]
    loads = [
        pltpu.make_async_copy(kvd.at[j], dkv.at[0], msem.at[0]),
        pltpu.make_async_copy(w, w_buf.at[0], msem.at[1]),
        pltpu.make_async_copy(wother, w_buf.at[1], msem.at[2]),
        pltpu.make_async_copy(tok, tok_buf, msem.at[3]),
        pltpu.make_async_copy(cot, cot_buf, msem.at[4]),
    ]
    for cp in loads:
        cp.start()
    meet([partner, xp, xm, zp, zm] + yfar)
    firsts, seconds = [], []
    for f in range(2):
        on_z, on_x = (z, zp, zm), (x, xp, xm)
        a, b = (on_z, on_x) if f == 0 else (on_x, on_z)
        if f == 0:
            pick, half = lambda m: (EVERY, m), lambda m, h: (h, m)
        else:
            pick, half = lambda m: (EVERY, EVERY, m), lambda m, h: (h, EVERY, m)
        firsts.append(
            RingReduce(*a, gkv.at[f], pick, half, relay.at[f], recv.at[f], ss, rs, (f, 0))
        )
        seconds.append(
            RingReduce(
                *b, mid.at[f], lambda m: (EVERY, m), lambda m, h: (h, m),
                relay2.at[f], recv2.at[f], ss, rs, (f, 1),
            )
        )
    q2 = RingReduce(
        x, xp, xm, q_mid, lambda m: (EVERY, m), lambda m, h: (h, m), q_relay, q_recv, ss, rs, (2, 0)
    )
    give = remote(kvd.at[1 - j], dkv.at[1], dsem.at[0], dsem.at[1], partner)
    give.start()
    q2.start()
    for ring in firsts:
        ring.start()
    for cp in loads:
        cp.wait()
    give.wait_recv()

    def tiles(first, last):
        @pl.loop(first, last)
        def _(n):
            total = None
            for half in range(2):
                lhs = jnp.concatenate([dq[half], dkv[half]], axis=-1)
                rhs = jnp.concatenate(
                    [w_buf[half, b, rows_at(512 * n, 512), :] for b in range(8)], axis=-1
                )
                term = lax.dot_general(
                    lhs, rhs, (((1,), (1,)), ((), ())), preferred_element_type=F32
                )
                total = term if total is None else total + term
            acc[n] = total

    def norm_rows(first, last):
        @pl.loop(first, last)
        def _(k):
            at = rows_at(k * 16, 16)
            t = tok_buf[at, :].astype(F32)
            grad = jnp.concatenate([acc[m, at, :] for m in range(5)], axis=-1)
            h = grad * gain[...]
            scale = lax.rsqrt(jnp.mean(t * t, axis=-1, keepdims=True) + EPS)
            inner = jnp.mean(h * t, axis=-1, keepdims=True)
            back = scale * h - t * (scale * scale * scale * inner)
            out[at, :] = (cot_buf[at, :].astype(F32) + back).astype(BF16)

    tiles(0, 1)
    q2.forward()
    tiles(1, 2)
    for ring in firsts:
        ring.forward()
    tiles(2, 4)
    q_end[...] = q2.finish().astype(BF16)
    q_sends = []
    for h in range(2):
        for i in range(2):
            goal = 2 * j + h
            q_sends.append(
                (
                    q_end.at[h, pl.ds(80 * i, 80)],
                    y,
                    dev(goal, z, x, i),
                    jnp.logical_and(goal == y, i == j),
                )
            )
    send_last(q_end, q_land, q_sends, ls.at[1], lr.at[1], lc.at[1], True)
    tiles(4, 5)
    for f in range(2):
        mid[f] = firsts[f].finish().astype(BF16)
        seconds[f].start()
    norm_rows(0, 12)
    for ring in seconds:
        ring.forward()
    norm_rows(12, 24)
    sends = []
    for f in range(2):
        end[f] = seconds[f].finish().astype(BF16)
        for h in range(2):
            goal = 2 * j + h
            sends.append(
                (end.at[f, h], y, dev(goal, z, x, f), jnp.logical_and(goal == y, f == j))
            )
    send_last(end, land, sends, ls.at[0], lr.at[0], lc.at[0], True)
    mine = lax.div(y, 2) == j
    send_last(q_end, q_land, q_sends, ls.at[1], lr.at[1], lc.at[1], False)
    sum_last(q_end.at[0, pl.ds(0, 80)], q_land, ls.at[1], lr.at[1], y, mine, partner, oq)
    send_last(end, land, sends, ls.at[0], lr.at[0], lc.at[0], False)
    sum_last(end.at[0, 0], land, ls.at[0], lr.at[0], y, mine, partner, okv)
    for ring in firsts + seconds + [q2]:
        ring.drain()
    give.wait_send()


def finish(gkv, kvd, dq, q_mid, w, wother, tok, cot, gain):
    return comm_call(
        finish_kernel,
        "finish",
        3,
        (sds((80, 256), F32), sds((80, 256), F32), sds((ROWS, D), BF16)),
        [
            pltpu.VMEM((2, ROWS, 512), BF16),
            pltpu.VMEM((2, 8, D, 128), BF16),
            pltpu.VMEM((ROWS, D), BF16),
            pltpu.VMEM((ROWS, D), BF16),
            pltpu.VMEM((5, ROWS, 512), F32),
            pltpu.VMEM((2, 2, 4, 80, 256), BF16),
            pltpu.VMEM((2, 2, 2, 4, 80, 256), BF16),
            pltpu.VMEM((2, 2, 4, 80, 256), BF16),
            pltpu.VMEM((2, 2, 80, 256), BF16),
            pltpu.VMEM((2, 2, 2, 80, 256), BF16),
            pltpu.VMEM((2, 2, 80, 256), BF16),
            pltpu.VMEM((4, 80, 256), BF16),
            pltpu.VMEM((2, 160, 256), BF16),
            pltpu.VMEM((2, 2, 160, 256), BF16),
            pltpu.VMEM((2, 160, 256), BF16),
            pltpu.VMEM((4, 80, 256), BF16),
            DMA((3, 2, 4)),
            DMA((3, 2, 4)),
            DMA((2, 4)),
            DMA((2, 4)),
            DMA((2,)),
            DMA((2,)),
            DMA((5,)),
        ],
        "vvvvhhhhv",
        "vvv",
    )(gkv, kvd, dq, q_mid, w, wother, tok, cot, gain)


def per_device(
    tokens,
    doc_ids,
    cotangent,
    input_gain,
    query_weight,
    key_weight,
    value_weight,
    output_weight,
    query_gain,
    key_gain,
    post_gain,
):
    seq_count, shard_size, width = tokens.shape
    c = lax.axis_index("ctx")
    core = lax.rem(c, 2)
    tok = tokens.reshape(ROWS, D)
    cot = cotangent.reshape(ROWS, D)
    wide = tok.astype(F32)
    scale = lax.rsqrt(jnp.mean(wide * wide, axis=-1, keepdims=True) + EPS)
    normed = (wide * scale * input_gain).astype(BF16)
    line = jnp.pad(doc_ids.reshape(1, ROWS).astype(BF16), ((0, 0), (0, D - ROWS)))
    at = lax.broadcasted_iota(jnp.int32, (NOTE_ROWS, 1), 0)
    notes = jnp.where(at == 8 * core, line, jnp.zeros((), BF16))
    noted = jnp.concatenate([normed, notes], axis=0)

    start = lax.div(c, 2) * 256
    positions = (start + jnp.arange(256, dtype=jnp.int32)).astype(F32)
    exponents = jnp.arange(128, dtype=jnp.int32).astype(F32) * (2.0 / 256)
    angles = positions[:, None] * ROPE_BASE ** (-exponents)

    def table(values):
        values = values.reshape(2, 1, 128, 128)
        return jnp.broadcast_to(values, (2, 3, 128, 128)).reshape(2 * ROWS, 128)

    cos, sin = table(jnp.cos(angles)), table(jnp.sin(angles))
    gains = jnp.pad(jnp.stack([query_gain, key_gain]), ((0, 6), (0, 0)))
    base = jnp.full((8, 128), start, jnp.int32)

    n2, w = gather(noted, query_weight, key_weight, value_weight)
    q, unit, raw = project(n2, w, cos, sin, gains)
    halo, wo, wother = exchange_halo(unit, output_weight.reshape(2, 128, D), w)
    layer_out, own, parts, qd, o_mid, gq = middle(
        q, unit, halo, base, wo.reshape(1024, D), tok, cot, post_gain.reshape(1, D),
        raw, cos, sin, gains, n2,
    )
    total, oo, q_mid, dq = return_grads(parts, own, o_mid, gq, qd.reshape(2, ROWS, 512))
    gkv, kvd = key_grads(n2, total.reshape(2 * ROWS, 512), raw, cos, sin, gains)
    okv, oq, tokens_grad = finish(
        gkv, kvd.reshape(2, ROWS, 512), dq, q_mid, w, wother, tok, cot, input_gain.reshape(1, D)
    )
    shape = (seq_count, shard_size, width)
    return (
        layer_out.reshape(shape),
        tokens_grad.reshape(shape),
        oq,
        okv[:, :128],
        okv[:, 128:],
        oo,
    )


def solution(mesh):
    placed = (
        P("fsdp", "ctx", None),
        P("fsdp", "ctx"),
        P("fsdp", "ctx", None),
        P(),
        P("fsdp", None),
        P("fsdp", None),
        P("fsdp", None),
        P("fsdp", None),
        P(),
        P(),
        P(),
    )
    return jax.shard_map(
        per_device,
        mesh=mesh,
        in_specs=placed,
        out_specs=(
            P("fsdp", "ctx", None),
            P("fsdp", "ctx", None),
            P("ctx", "fsdp"),
            P("ctx", "fsdp"),
            P("ctx", "fsdp"),
            P("ctx", "fsdp"),
        ),
        check_vma=False,
    )
```

```python
import functools

import jax
import jax.numpy as jnp
from jax import lax
from jax.experimental import pallas as pl
from jax.experimental.pallas import tpu as pltpu
from jax.sharding import PartitionSpec as P

EPS = 1e-06
ROPE_BASE = 10000.0
Q_FACTOR = 0.0625
WINDOW = 1024
F32 = jnp.float32
BF16 = jnp.bfloat16
MESH = pl.DeviceIdType.MESH
VMEM_LIMIT = 64 * 1024 * 1024 - 512 * 1024

D = 2560
ROWS = 384
NOTE_ROWS = 16
UNIT = 2 * ROWS + NOTE_ROWS


def place():
    y = lax.axis_index("fsdp")
    c = lax.axis_index("ctx")
    j = lax.rem(c, 2)
    zx = lax.div(c, 2)
    return y, lax.div(zx, 4), lax.rem(zx, 4), j


def dev(y, z, x, j):
    return (y, (z * 4 + x) * 2 + j)


def up(a, n=1):
    return lax.rem(a + n, 4)


def remote(src, dst, ss, rs, device):
    return pltpu.make_async_remote_copy(
        src_ref=src, dst_ref=dst, send_sem=ss, recv_sem=rs, device_id=device, device_id_type=MESH
    )


def meet(devices):
    barrier = pltpu.get_barrier_semaphore()
    for device in devices:
        pl.semaphore_signal(barrier, inc=1, device_id=device, device_id_type=MESH)
    pl.semaphore_wait(barrier, len(devices))


def rows_at(start, size, unit=16):
    return pl.ds(pl.multiple_of(start, unit), size)


def vmem(n):
    return [pl.BlockSpec(memory_space=pltpu.VMEM)] * n


def spaces(kinds):
    where = {"v": pltpu.VMEM, "h": pl.ANY}
    return [pl.BlockSpec(memory_space=where[kind]) for kind in kinds]


def comm_call(kernel, name, cid, out_shape, scratch, ins, outs):
    return pl.pallas_call(
        kernel,
        name=name,
        out_shape=list(out_shape),
        in_specs=spaces(ins),
        out_specs=spaces(outs),
        scratch_shapes=scratch,
        compiler_params=pltpu.CompilerParams(
            collective_id=cid, has_side_effects=True, vmem_limit_bytes=VMEM_LIMIT
        ),
    )


def sds(shape, dtype):
    return jax.ShapeDtypeStruct(shape, dtype)


DMA = pltpu.SemaphoreType.DMA


class RingGather:
    def __init__(self, me, plus, minus, region, half, ss, rs, index):
        self.me, self.plus, self.minus = me, plus, minus
        self.region, self.half, self.ss, self.rs, self.index = region, half, ss, rs, index

    def _copy(self, ref, k, device):
        at = self.index + (k,)
        return remote(ref, ref, self.ss.at[at], self.rs.at[at], device)

    def start(self):
        self._copy(self.region(self.me), 0, self.plus).start()
        self._copy(self.region(self.me), 1, self.minus).start()

    def forward(self):
        left, right = up(self.me, 3), up(self.me, 1)
        self._copy(self.region(left), 0, self.plus).wait_recv()
        self._copy(self.half(left, 0), 2, self.plus).start()
        self._copy(self.region(right), 1, self.minus).wait_recv()
        self._copy(self.half(right, 1), 3, self.minus).start()

    def finish(self):
        far = up(self.me, 2)
        self._copy(self.half(far, 0), 2, self.plus).wait_recv()
        self._copy(self.half(far, 1), 3, self.minus).wait_recv()

    def drain(self):
        self._copy(self.region(self.me), 0, self.plus).wait_send()
        self._copy(self.region(self.me), 1, self.minus).wait_send()
        self._copy(self.half(up(self.me, 3), 0), 2, self.plus).wait_send()
        self._copy(self.half(up(self.me, 1), 1), 3, self.minus).wait_send()


PLANE = 96


def gather_kernel(n_ref, wq, wk, wv, n2, w, lsem, nsem, ysend, yrecv, gsend, grecv, rsend, rrecv):
    y, z, x, j = place()
    partner = dev(y, z, x, 1 - j)
    xp, xm = dev(y, z, up(x), j), dev(y, z, up(x, 3), j)
    zp, zm = dev(y, up(z), x, j), dev(y, up(z, 3), x, j)
    ys = [dev(up(y, r), z, x, j) for r in (1, 2, 3)]
    own = rows_at(640 * y, 640)
    local = []
    for b in range(8):
        if b < 4:
            src = wq.at[:, pl.ds(pl.multiple_of(512 * j + 128 * b, 128), 128)]
        elif b < 6:
            src = wk.at[:, pl.ds(pl.multiple_of(256 * j + 128 * (b - 4), 128), 128)]
        else:
            src = wv.at[:, pl.ds(pl.multiple_of(256 * j + 128 * (b - 6), 128), 128)]
        local.append(pltpu.make_async_copy(src, w.at[b, own], lsem.at[b]))
    local.append(pltpu.make_async_copy(n_ref, n2.at[j], lsem.at[8]))
    for cp in local:
        cp.start()
    meet([partner, xp, xm, zp, zm] + ys)
    for cp in local[:8]:
        cp.wait()

    def piece_q(yy):
        return w.at[x, rows_at(640 * yy + PLANE * z, PLANE)]

    def piece_k(yy):
        return w.at[4 + z, rows_at(640 * yy + PLANE * x, PLANE)]

    straight = RingGather(
        y,
        ys[0],
        ys[2],
        lambda m: w.at[:, rows_at(640 * m + 4 * PLANE, 640 - 4 * PLANE)],
        lambda m, h: w.at[pl.ds(4 * h, 4), rows_at(640 * m + 4 * PLANE, 640 - 4 * PLANE)],
        rsend,
        rrecv,
        (),
    )

    first = []
    for r in range(3):
        for f, piece in enumerate((piece_q, piece_k)):
            cp = remote(piece(y), piece(y), ysend.at[f, r], yrecv.at[f, r], ys[r])
            cp.start()
            first.append((cp, f, r, piece))
    straight.start()
    swap = remote(n_ref, n2.at[j], nsem.at[0], nsem.at[1], partner)
    swap.start()

    def ring(f, stage, r):
        yy = up(y, 3 - r)
        first, count = 4 * f, PLANE // 2
        if stage == 0:
            inner = z if f == 0 else x
            region = lambda m: w.at[first + m, rows_at(640 * yy + PLANE * inner, PLANE)]
            half = lambda m, h: w.at[
                first + m, rows_at(640 * yy + PLANE * inner + count * h, count)
            ]
        else:
            region = lambda m: w.at[pl.ds(first, 4), rows_at(640 * yy + PLANE * m, PLANE)]
            half = lambda m, h: w.at[
                pl.ds(first + 2 * h, 2), rows_at(640 * yy + PLANE * m, PLANE)
            ]
        on_x = (f + stage) % 2 == 0
        me, plus, minus = (x, xp, xm) if on_x else (z, zp, zm)
        return RingGather(me, plus, minus, region, half, gsend, grecv, (f, stage, r))

    rings = [[[ring(f, s, r) for r in range(3)] for s in range(2)] for f in range(2)]
    for cp, f, r, piece in first:
        yy = up(y, 3 - r)
        remote(piece(yy), piece(yy), ysend.at[f, r], yrecv.at[f, r], ys[r]).wait_recv()
        rings[f][0][r].start()
    for r in range(3):
        for f in range(2):
            rings[f][0][r].forward()
    for r in range(3):
        for f in range(2):
            rings[f][0][r].finish()
            rings[f][1][r].start()
    straight.forward()
    for r in range(3):
        for f in range(2):
            rings[f][1][r].forward()
    for r in range(3):
        for f in range(2):
            rings[f][1][r].finish()
    for r in range(3):
        for f in range(2):
            rings[f][0][r].drain()
            rings[f][1][r].drain()
    straight.finish()
    straight.drain()
    for cp, f, r, piece in first:
        cp.wait_send()
    swap.wait()
    local[8].wait()


def gather(noted, wq, wk, wv):
    return comm_call(
        gather_kernel,
        "gather_weights",
        0,
        (sds((2, ROWS + NOTE_ROWS, D), BF16), sds((8, D, 128), BF16)),
        [
            DMA((9,)),
            DMA((2,)),
            DMA((2, 3)),
            DMA((2, 3)),
            DMA((2, 2, 3, 4)),
            DMA((2, 2, 3, 4)),
            DMA((4,)),
            DMA((4,)),
        ],
        "vvvv",
        "hh",
    )(noted, wq, wk, wv)


def project_kernel(n2, w, cos, sin, gains, q_out, unit, raw_out):
    n = pl.program_id(0)
    rows = n2[:, :ROWS, :].reshape(2 * ROWS, D)
    weight = jnp.concatenate([w[0], w[1]], axis=-1)
    acc = jnp.dot(rows, weight, preferred_element_type=F32)

    def rotated(gain, factor):
        scale = lax.rsqrt(jnp.mean(acc * acc, axis=-1, keepdims=True) + EPS)
        normed = acc * scale * gain
        a, b = normed[:, :128], normed[:, 128:]
        c, s = cos[...], sin[...]
        return (jnp.concatenate([a * c - b * s, b * c + a * s], axis=-1) * factor).astype(BF16)

    @pl.when(n < 3)
    def _():
        raw_out[0] = acc

    @pl.when(n < 2)
    def _():
        q_out[0] = rotated(gains[0:1, :], Q_FACTOR)

    @pl.when(n == 2)
    def _():
        unit[0 : 2 * ROWS, 0:256] = rotated(gains[1:2, :], 1.0)

    @pl.when(n == 3)
    def _():
        unit[0 : 2 * ROWS, 256:512] = acc.astype(BF16)
        unit[2 * ROWS : UNIT, :] = n2[0, ROWS:, 0:512] + n2[1, ROWS:, 0:512]


def project(n2, w, cos, sin, gains):
    return pl.pallas_call(
        project_kernel,
        name="project",
        grid=(4,),
        in_specs=[
            pl.BlockSpec((2, ROWS + NOTE_ROWS, D), lambda n: (0, 0, 0)),
            pl.BlockSpec((2, D, 128), lambda n: (n, 0, 0)),
            pl.BlockSpec((2 * ROWS, 128), lambda n: (0, 0)),
            pl.BlockSpec((2 * ROWS, 128), lambda n: (0, 0)),
            pl.BlockSpec((8, 256), lambda n: (0, 0)),
        ],
        out_specs=[
            pl.BlockSpec((1, 2 * ROWS, 256), lambda n: (jnp.minimum(n, 1), 0, 0)),
            pl.BlockSpec((UNIT, 512), lambda n: (0, 0)),
            pl.BlockSpec((1, 2 * ROWS, 256), lambda n: (jnp.minimum(n, 2), 0, 0)),
        ],
        out_shape=[
            sds((2, 2 * ROWS, 256), BF16),
            sds((UNIT, 512), BF16),
            sds((3, 2 * ROWS, 256), F32),
        ],
        compiler_params=pltpu.CompilerParams(vmem_limit_bytes=VMEM_LIMIT),
    )(n2, w, cos, sin, gains)


HALO_CHUNKS = 7
HALO_ROWS = UNIT // HALO_CHUNKS


def halo_kernel(unit, wo_own, w, halo, wo, wother, hsend, hrecv, osend, orecv, lsem, wsem):
    y, z, x, j = place()
    partner = dev(y, z, x, 1 - j)
    xp, xm = dev(y, z, up(x), j), dev(y, z, up(x, 3), j)
    zp, zm = dev(y, up(z), x, j), dev(y, up(z, 3), x, j)
    yp, ym = dev(up(y), z, x, j), dev(up(y, 3), z, x, j)
    ocopy = pltpu.make_async_copy(wo_own, wo.at[y], lsem.at[1])
    ocopy.start()
    meet([partner, xp, xm, zp, zm, yp, ym])

    def rows(k):
        return rows_at(k * HALO_ROWS, HALO_ROWS)

    def shift(k):
        return remote(unit.at[rows(k)], halo.at[3, rows(k)], hsend.at[0, k], hrecv.at[0, k], zp)

    def right(src, k):
        return remote(src.at[rows(k)], halo.at[0, rows(k)], hsend.at[1, k], hrecv.at[1, k], xp)

    def left(src, k):
        return remote(src.at[rows(k)], halo.at[2, rows(k)], hsend.at[2, k], hrecv.at[2, k], xm)

    def far_right(k):
        return remote(
            halo.at[0, rows(k)], halo.at[1, rows(k)], hsend.at[3, k], hrecv.at[3, k], xp
        )

    def far_left(k):
        return remote(
            halo.at[2, rows(k)], halo.at[1, rows(k)], hsend.at[4, k], hrecv.at[3, k], xm
        )

    before = halo.at[3]
    inner = jnp.logical_and(x > 0, x < 3)

    @pl.loop(0, HALO_CHUNKS)
    def _(k):
        shift(k).start()

        @pl.when(x < 3)
        def _():
            right(unit, k).start()

        @pl.when(x == 0)
        def _():
            left(unit, k).start()

    ocopy.wait()
    ring = RingGather(
        y,
        yp,
        ym,
        lambda m: wo.at[m, j],
        lambda m, h: wo.at[m, j, pl.ds(64 * h, 64)],
        osend,
        orecv,
        (0,),
    )
    ring.start()
    swap = remote(w, wother, wsem.at[0], wsem.at[1], partner)
    swap.start()

    def step(k):
        shift(k).wait_recv()

        @pl.when(x == 3)
        def _():
            right(before, k).start()

        @pl.when(x > 0)
        def _():
            left(before, k).start()

        right(unit, k).wait_recv()

        @pl.when(inner)
        def _():
            far_right(k).start()

        @pl.when(k > 0)
        def _():
            left(unit, k - 1).wait_recv()

            @pl.when(inner)
            def _():
                far_left(k - 1).start()

    pl.loop(0, 4)(step)
    ring.forward()
    share = []

    def give(n, m):
        cp = remote(wo.at[m, j], wo.at[m, j], osend.at[1, n], orecv.at[1, n], partner)
        cp.start()
        share.append(cp)

    give(0, up(y, 3))
    give(1, up(y, 1))
    pl.loop(4, HALO_CHUNKS)(step)
    left(unit, HALO_CHUNKS - 1).wait_recv()

    @pl.when(inner)
    def _():
        far_left(HALO_CHUNKS - 1).start()

    ring.finish()
    give(2, up(y, 2))
    for n, m in enumerate((up(y, 3), up(y, 1), up(y, 2))):
        remote(
            wo.at[m, 1 - j], wo.at[m, 1 - j], osend.at[1, n], orecv.at[1, n], partner
        ).wait_recv()
    for cp in share:
        cp.wait_send()
    ring.drain()

    @pl.loop(0, HALO_CHUNKS)
    def _(k):
        far_right(k).wait_recv()
        shift(k).wait_send()
        right(unit, k).wait_send()
        left(unit, k).wait_send()

        @pl.when(inner)
        def _():
            far_right(k).wait_send()
            far_left(k).wait_send()

    swap.wait()


def exchange_halo(unit, wo_own, w):
    return comm_call(
        halo_kernel,
        "exchange_halo",
        1,
        (
            sds((4, UNIT, 512), BF16),
            sds((4, 2, 128, D), BF16),
            sds((8, D, 128), BF16),
        ),
        [
            DMA((5, HALO_CHUNKS)),
            DMA((4, HALO_CHUNKS)),
            DMA((2, 4)),
            DMA((2, 4)),
            DMA((2,)),
            DMA((2,)),
        ],
        "vvh",
        "hhh",
    )(unit, wo_own, w)


KEYS = 1280


def window_of(unit, halo, s, first, last):
    parts = []
    for d in (4, 3, 2, 1, 0):
        for i in range(2):
            at = rows_at(i * ROWS + s * 128, 128)
            if d == 0:
                parts.append(unit[at, first:last])
            else:
                parts.append(halo[d - 1, at, first:last])
    return jnp.concatenate(parts, axis=0)


def map_back(upstream, raw, c, s, gain, factor):
    a, b = upstream[:, :128] * factor, upstream[:, 128:] * factor
    turned = jnp.concatenate([a * c + b * s, b * c - a * s], axis=-1) * gain
    scale = lax.rsqrt(jnp.mean(raw * raw, axis=-1, keepdims=True) + EPS)
    inner = jnp.mean(turned * raw, axis=-1, keepdims=True)
    return scale * turned - raw * (scale * scale * scale * inner)


def add_into(ref, at, other):
    ref[at] = (ref[at].astype(F32) + other.astype(F32)).astype(BF16)


class RingReduce:
    def __init__(self, me, plus, minus, data, pick, half, relay, recv, ss, rs, index):
        self.me, self.plus, self.minus = me, plus, minus
        self.data, self.pick, self.half = data, pick, half
        self.relay, self.recv, self.ss, self.rs, self.index = relay, recv, ss, rs, index

    def _copy(self, src, dst, k, device):
        at = self.index + (k,)
        return remote(src, dst, self.ss.at[at], self.rs.at[at], device)

    def _first(self):
        far = up(self.me, 2)
        return (
            self._copy(self.data.at[self.half(far, 0)], self.relay.at[0], 0, self.plus),
            self._copy(self.data.at[self.half(far, 1)], self.relay.at[1], 1, self.minus),
        )

    def _second(self):
        right, left = up(self.me, 1), up(self.me, 3)
        return (
            self._copy(self.data.at[self.pick(right)], self.recv.at[0], 2, self.plus),
            self._copy(self.data.at[self.pick(left)], self.recv.at[1], 3, self.minus),
        )

    def start(self):
        for cp in self._first():
            cp.start()

    def forward(self):
        a, b = self._first()
        c, d = self._second()
        a.wait_recv()
        add_into(self.data, self.half(up(self.me, 1), 0), self.relay[0])
        c.start()
        b.wait_recv()
        add_into(self.data, self.half(up(self.me, 3), 1), self.relay[1])
        d.start()

    def finish(self):
        c, d = self._second()
        c.wait_recv()
        d.wait_recv()
        return (
            self.data[self.pick(self.me)].astype(F32)
            + self.recv[0].astype(F32)
            + self.recv[1].astype(F32)
        )

    def drain(self):
        for cp in self._first() + self._second():
            cp.wait_send()


def middle_kernel(
    q, unit, halo, base, wo_h, tok_h, cot_h, gain,
    layer_out, grad, go, soft_h,
    wo, tok, cot, soft, att, attx, proj, gp2, grad_send,
    loadsem, keepsem, asend, arecv, gsend, grecv, dsem,
):
    y, z, x, j = place()
    partner = dev(y, z, x, 1 - j)
    loads = [
        pltpu.make_async_copy(src, dst, loadsem.at[n])
        for n, (src, dst) in enumerate(
            ((wo_h, wo), (tok_h, tok), (cot_h, cot))
        )
    ]
    for cp in loads:
        cp.start()
    meet([partner])

    def keep_soft(s):
        return pltpu.make_async_copy(soft.at[s], soft_h.at[s], keepsem.at[s])

    def give_attended(s):
        return remote(att.at[1 - j, s], attx.at[s], asend.at[s], arecv.at[s], partner)

    key_at = lax.broadcasted_iota(jnp.int32, (256, KEYS), 1) - WINDOW
    query_at = lax.broadcasted_iota(jnp.int32, (256, KEYS), 0)

    @pl.loop(0, 3)
    def _(s):
        keys = window_of(unit, halo, s, 0, 256)
        values = window_of(unit, halo, s, 256, 512)
        lanes = pl.ds(pl.multiple_of(s * 128, 128), 128)
        notes = []
        for d in (4, 3, 2, 1, 0):
            block = unit[2 * ROWS :, lanes] if d == 0 else halo[d - 1, 2 * ROWS :, lanes]
            block = block.astype(F32)
            notes.extend([block[0:1], block[8:9]])
        key_docs = jnp.concatenate(notes, axis=-1)
        query_docs = jnp.concatenate(
            [jnp.transpose(jnp.broadcast_to(note, (128, 128))) for note in notes[8:]], axis=0
        )
        query_docs = jnp.concatenate([query_docs] * (KEYS // 128), axis=-1)
        allowed = (
            (query_docs == key_docs)
            & (key_at <= query_at)
            & (key_at > query_at - WINDOW)
            & (key_at + base[0:1, 0:1] >= 0)
        )
        for h in range(2):
            rows = q[h, :, s].reshape(256, 256)
            scores = lax.dot_general(
                rows, keys, (((1,), (1,)), ((), ())), preferred_element_type=F32
            )
            masked = jnp.where(allowed, scores, -1e30)
            highest = jnp.max(masked, axis=-1, keepdims=True)
            raised = jnp.exp(masked - highest)
            weights = (raised / jnp.sum(raised, axis=-1, keepdims=True)).astype(BF16)
            soft[s, 256 * h : 256 * h + 256, :] = weights
            out = jnp.dot(weights, values, preferred_element_type=F32).astype(BF16)
            att[:, s, :, 256 * h : 256 * h + 256] = out.reshape(2, 128, 256)
        give_attended(s).start()
        keep_soft(s).start()

    for cp in loads:
        cp.wait()
    for s in range(3):
        give_attended(s).wait_recv()
    mine, others = att[j].reshape(ROWS, 512), attx[...].reshape(ROWS, 512)
    own_heads, other_heads = rows_at(512 * j, 512), rows_at(512 * (1 - j), 512)

    @pl.loop(0, 5)
    def _(n):
        cols = pl.ds(pl.multiple_of(512 * n, 512), 512)
        proj[:, cols] = jnp.dot(
            mine, wo[own_heads, cols], preferred_element_type=F32
        ) + jnp.dot(others, wo[other_heads, cols], preferred_element_type=F32)

    def give_projected(t):
        at = pl.ds(128 * t, 128)
        return remote(gp2.at[0, at], gp2.at[1, at], gsend.at[t], grecv.at[t], partner)

    for t in range(3):

        @pl.loop(8 * t, 8 * t + 8)
        def _(k):
            at = rows_at(k * 16, 16)
            p = proj[at, :]
            g = gain[...]
            scale = lax.rsqrt(jnp.mean(p * p, axis=-1, keepdims=True) + EPS)
            layer_out[at, :] = (tok[at, :].astype(F32) + p * scale * g).astype(BF16)
            h = cot[at, :].astype(F32) * g
            inner = jnp.mean(h * p, axis=-1, keepdims=True)
            gp2[0, at, :] = (scale * h - p * (scale * scale * scale * inner)).astype(BF16)

        give_projected(t).start()

    upstream = gp2[0]

    def attended_grad(heads):
        part = lax.dot_general(
            upstream, wo[heads, :], (((1,), (1,)), ((), ())), preferred_element_type=F32
        )
        return part.astype(BF16).reshape(3, 128, 512)

    grad_send[...] = attended_grad(other_heads)
    give_grad = remote(grad_send, grad.at[j], dsem.at[0], dsem.at[1], partner)
    give_grad.start()
    grad[j] = attended_grad(own_heads)
    for t in range(3):
        give_projected(t).wait_recv()
    across = (((0,), (0,)), ((), ()))
    other_rows = att[1 - j].reshape(ROWS, 512)
    for n in range(4):
        cols = slice(640 * n, 640 * n + 640)
        term = lax.dot_general(
            mine, gp2[0, :, cols], across, preferred_element_type=F32
        ) + lax.dot_general(other_rows, gp2[1, :, cols], across, preferred_element_type=F32)
        go[n] = term.astype(BF16).reshape(2, 4, 64, 640)
    give_grad.wait_recv()
    for s in range(3):
        give_attended(s).wait_send()
        give_projected(s).wait_send()
        keep_soft(s).wait()
    give_grad.wait_send()


def middle(q, unit, halo, base, wo, tok, cot, gain):
    return comm_call(
        middle_kernel,
        "middle",
        4,
        (
            sds((ROWS, D), BF16),
            sds((2, 3, 128, 512), BF16),
            sds((4, 2, 4, 64, 640), BF16),
            sds((3, 512, KEYS), BF16),
        ),
        [
            pltpu.VMEM((1024, D), BF16),
            pltpu.VMEM((ROWS, D), BF16),
            pltpu.VMEM((ROWS, D), BF16),
            pltpu.VMEM((3, 512, KEYS), BF16),
            pltpu.VMEM((2, 3, 128, 512), BF16),
            pltpu.VMEM((3, 128, 512), BF16),
            pltpu.VMEM((ROWS, D), F32),
            pltpu.VMEM((2, ROWS, D), BF16),
            pltpu.VMEM((3, 128, 512), BF16),
            DMA((3,)),
            DMA((3,)),
            DMA((3,)),
            DMA((3,)),
            DMA((3,)),
            DMA((3,)),
            DMA((2,)),
        ],
        "vvvvhhhv",
        "vvvh",
    )(q.reshape(2, 2, 3, 128, 256), unit, halo, base, wo, tok, cot, gain)


EVERY = slice(None)


def send_last(end, land, sends, ls, lr, lc, start):
    for n, (src, slot, device, here) in enumerate(sends):

        @pl.when(here)
        def _():
            cp = pltpu.make_async_copy(src, land.at[slot], lc)
            if start:
                cp.start()
            else:
                cp.wait()

        @pl.when(jnp.logical_not(here))
        def _():
            cp = remote(src, land.at[slot], ls.at[n], lr.at[slot], device)
            if start:
                cp.start()
            else:
                cp.wait_send()


def sum_last(like, land, ls, lr, me, mine, partner, out):
    for m in range(4):

        @pl.when(jnp.logical_not(jnp.logical_and(m == me, mine)))
        def _():
            remote(like, land.at[m], ls.at[0], lr.at[m], partner).wait_recv()

    out[...] = (land[0].astype(F32) + land[1].astype(F32)) + (
        land[2].astype(F32) + land[3].astype(F32)
    )


TAIL = dict(
    own=((2, 3, 128, 512), F32),
    parts=((4, 2, 3, 128, 512), BF16),
    qd=((2, 3, 128, 512), BF16),
    dq=((3, 128, 512), BF16),
    kvd=((2, 3, 128, 512), BF16),
    dkv=((3, 128, 512), BF16),
    n2=((2, ROWS + NOTE_ROWS, D), BF16),
    raw_k=((2, 3, 128, 256), F32),
    gq=((2, 4, 4, 160, 256), BF16),
    gkv=((2, 2, 4, 4, 80, 256), BF16),
    relay=((2, 2, 3, 128, 512), BF16),
    near=((2, 2, 3, 128, 512), BF16),
    after=((2, 3, 128, 512), BF16),
    go=((4, 2, 4, 64, 640), BF16),
    o_relay=((2, 4, 64, 640), BF16),
    o_recv=((2, 2, 4, 64, 640), BF16),
    o_mid=((2, 4, 64, 640), BF16),
    o_relay2=((2, 64, 640), BF16),
    o_recv2=((2, 2, 64, 640), BF16),
    o_end=((2, 64, 640), BF16),
    o_land=((4, 32, 640), BF16),
    q_relay=((2, 4, 160, 256), BF16),
    q_recv=((2, 2, 4, 160, 256), BF16),
    q_mid=((2, 4, 160, 256), BF16),
    q_relay2=((2, 160, 256), BF16),
    q_recv2=((2, 2, 160, 256), BF16),
    q_end=((2, 160, 256), BF16),
    q_land=((4, 80, 256), BF16),
    k_relay=((2, 2, 4, 80, 256), BF16),
    k_recv=((2, 2, 2, 4, 80, 256), BF16),
    k_mid=((2, 2, 4, 80, 256), BF16),
    k_relay2=((2, 2, 80, 256), BF16),
    k_recv2=((2, 2, 2, 80, 256), BF16),
    k_end=((2, 2, 80, 256), BF16),
    k_land=((4, 80, 256), BF16),
)
TAIL_SEMS = dict(
    ssem=(5, 2, 3),
    rsem=(5, 2, 3),
    dsend=(2, 3),
    drecv=(2, 3),
    ss=(4, 2, 4),
    rs=(4, 2, 4),
    ls=(3, 4),
    lr=(3, 4),
    lc=(3,),
    load=(16,),
    keep=(3,),
    put=(2,),
)


def tail_kernel(
    q_h, unit_h, halo_h, soft_h, grad_h, raw_h, cos, sin, gains, go_h, n2_h,
    w_h, wother_h, tok_h, cot_h, gain,
    oo, oq, okv, out_h,
    *scratch,
):
    names = list(TAIL) + list(TAIL_SEMS)
    b = dict(zip(names, scratch))
    own, parts, qd, kvd = b["own"], b["parts"], b["qd"], b["kvd"]
    relay, near, after = b["relay"], b["near"], b["after"]
    ssem, rsem, ss, rs, load = b["ssem"], b["rsem"], b["ss"], b["rs"], b["load"]
    y, z, x, j = place()
    partner = dev(y, z, x, 1 - j)
    xp, xm = dev(y, z, up(x), j), dev(y, z, up(x, 3), j)
    zp, zm = dev(y, up(z), x, j), dev(y, up(z, 3), x, j)
    yp, ym = dev(up(y), z, x, j), dev(up(y, 3), z, x, j)
    yfar = [dev(up(y, r), z, x, i) for r in (1, 2, 3) for i in (0, 1)]
    zfar = [dev(y, up(z, r), x, i) for r in (1, 2, 3) for i in (0, 1)]
    inner = jnp.logical_and(x > 0, x < 3)
    low = x < 2
    across = (((0,), (0,)), ((), ()))
    apart = (((1,), (1,)), ((), ()))

    def get(src, dst, n):
        return pltpu.make_async_copy(src, dst, load.at[n])

    def relay_left(i, s):
        return remote(parts.at[1, i, s], relay.at[0, i, s], ssem.at[0, i, s], rsem.at[0, i, s], xm)

    def relay_right(i, s):
        return remote(parts.at[1, i, s], relay.at[1, i, s], ssem.at[1, i, s], rsem.at[1, i, s], xp)

    def to_left(i, s):
        return remote(parts.at[0, i, s], near.at[0, i, s], ssem.at[2, i, s], rsem.at[2, i, s], xm)

    def to_right(i, s):
        return remote(parts.at[2, i, s], near.at[1, i, s], ssem.at[3, i, s], rsem.at[3, i, s], xp)

    def back(i, s):
        return remote(parts.at[3, i, s], after.at[i, s], ssem.at[4, i, s], rsem.at[4, i, s], zm)

    def give_delta(f, s):
        src, dst = ((qd, b["dq"]), (kvd, b["dkv"]))[f]
        return remote(
            src.at[1 - j, s], dst.at[s], b["dsend"].at[f, s], b["drecv"].at[f, s], partner
        )

    rows_whole, rows_half = lambda m: (EVERY, m), lambda m, h: (h, m)
    o1 = RingReduce(
        y, yp, ym, b["go"], lambda m: (m,), lambda m, h: (m, h),
        b["o_relay"], b["o_recv"], ss, rs, (0, 0),
    )
    o2 = RingReduce(
        x, xp, xm, b["o_mid"], rows_whole, rows_half, b["o_relay2"], b["o_recv2"], ss, rs, (0, 1)
    )
    q1 = RingReduce(
        z, zp, zm, b["gq"], rows_whole, rows_half, b["q_relay"], b["q_recv"], ss, rs, (1, 0)
    )
    q2 = RingReduce(
        x, xp, xm, b["q_mid"], rows_whole, rows_half, b["q_relay2"], b["q_recv2"], ss, rs, (1, 1)
    )
    k1, k2 = [], []
    for f in range(2):
        first, second = ((z, zp, zm), (x, xp, xm))[:: 1 - 2 * f]
        if f == 0:
            pick, half = rows_whole, rows_half
        else:
            pick, half = lambda m: (EVERY, EVERY, m), lambda m, h: (h, EVERY, m)
        k1.append(
            RingReduce(
                *first, b["gkv"].at[f], pick, half,
                b["k_relay"].at[f], b["k_recv"].at[f], ss, rs, (2 + f, 0),
            )
        )
        k2.append(
            RingReduce(
                *second, b["k_mid"].at[f], rows_whole, rows_half,
                b["k_relay2"].at[f], b["k_recv2"].at[f], ss, rs, (2 + f, 1),
            )
        )

    def attention(q, unit, halo, soft, grad, raw):
        loads = [
            get(go_h, b["go"], 0),
            get(unit_h, unit, 1),
            get(halo_h, halo, 2),
            get(q_h, q, 3),
            get(grad_h, grad, 4),
            get(raw_h.at[pl.ds(0, 2)], raw, 5),
        ]

        def get_soft(s):
            return pltpu.make_async_copy(soft_h.at[s], soft.at[s], b["keep"].at[s])

        for cp in loads:
            cp.start()
        for s in range(3):
            get_soft(s).start()
        get(n2_h, b["n2"], 6).start()
        get(raw_h.at[2], b["raw_k"], 7).start()
        meet([partner, xp, xm] + yfar + zfar)
        loads[0].wait()
        o1.start()
        for cp in loads[1:]:
            cp.wait()

        def backward(first, last):
            @pl.loop(first, last)
            def _(s):
                get_soft(s).wait()
                keys = window_of(unit, halo, s, 0, 256)
                values = window_of(unit, halo, s, 256, 512)
                grads = jnp.concatenate(
                    [grad[:, s, :, 256 * h : 256 * h + 256].reshape(256, 256) for h in range(2)],
                    axis=0,
                )
                weights = soft[s]

                def emit(part, first_col):
                    for n, d in enumerate((4, 3, 2, 1, 0)):
                        for i in range(2):
                            piece = part[256 * n + 128 * i : 256 * n + 128 * i + 128]
                            cols = slice(first_col, first_col + 256)
                            if d == 0:
                                own[i, s, :, cols] = piece
                            else:
                                parts[d - 1, i, s, :, cols] = piece.astype(BF16)

                emit(lax.dot_general(weights, grads, across, preferred_element_type=F32), 256)
                grad_weights = lax.dot_general(
                    grads, values, apart, preferred_element_type=F32
                )
                wide = weights.astype(F32)
                moved = wide * grad_weights
                dots = jnp.sum(moved, axis=-1, keepdims=True)
                score_grads = (moved - wide * dots).astype(BF16)
                queries = jnp.concatenate(
                    [q[h, :, s].reshape(256, 256) for h in range(2)], axis=0
                )
                emit(
                    lax.dot_general(score_grads, queries, across, preferred_element_type=F32), 0
                )
                for i in range(2):

                    @pl.when(low)
                    def _():
                        relay_right(i, s).start()

                    @pl.when(jnp.logical_not(low))
                    def _():
                        relay_left(i, s).start()

                    @pl.when(jnp.logical_not(inner))
                    def _():
                        to_left(i, s).start()
                        to_right(i, s).start()

                grad_queries = jnp.dot(score_grads, keys, preferred_element_type=F32)
                c, sn = cos[:, s].reshape(256, 128), sin[:, s].reshape(256, 128)
                for h in range(2):
                    turned = map_back(
                        grad_queries[256 * h : 256 * h + 256],
                        raw[h, :, s].reshape(256, 256),
                        c,
                        sn,
                        gains[0:1, :],
                        Q_FACTOR,
                    )
                    qd[:, s, :, 256 * h : 256 * h + 256] = turned.astype(BF16).reshape(2, 128, 256)
                give_delta(0, s).start()

        backward(0, 2)
        o1.forward()
        backward(2, 3)

    pl.run_scoped(
        attention,
        pltpu.VMEM((2, 2, 3, 128, 256), BF16),
        pltpu.VMEM((UNIT, 512), BF16),
        pltpu.VMEM((4, UNIT, 512), BF16),
        pltpu.VMEM((3, 512, KEYS), BF16),
        pltpu.VMEM((2, 3, 128, 512), BF16),
        pltpu.VMEM((2, 2, 3, 128, 256), F32),
    )

    def relay_step(s):
        @pl.when(inner)
        def _():
            for i in range(2):
                relay_left(i, s).wait_recv()
                add_into(parts, (0, i, s), relay[0, i, s])
                to_left(i, s).start()
                relay_right(i, s).wait_recv()
                add_into(parts, (2, i, s), relay[1, i, s])
                to_right(i, s).start()

    def near_step(s):
        for i in range(2):
            to_left(i, s).wait_recv()
            to_right(i, s).wait_recv()
            from_right = near[0, i, s].astype(F32)
            from_left = near[1, i, s].astype(F32)
            zero = jnp.zeros_like(from_left)
            near_a = jnp.where(x < 3, from_right, zero) + jnp.where(x == 0, from_left, zero)
            near_b = jnp.where(x == 3, from_right, zero) + jnp.where(x > 0, from_left, zero)
            add_into(parts, (3, i, s), near_b)
            back(i, s).start()
            own[i, s] = own[i, s] + near_a

    def total_step(s):
        for i in range(2):
            back(i, s).wait_recv()
            total = own[i, s] + after[i, s].astype(F32)
            kd = map_back(
                total[:, :256], b["raw_k"][i, s], cos[i, s], sin[i, s], gains[1:2, :], 1.0
            )
            kvd[i, s, :, 0:256] = kd.astype(BF16)
            kvd[i, s, :, 256:512] = total[:, 256:].astype(BF16)
        give_delta(1, s).start()

    def rows_of(zz):
        cols = pl.ds(pl.multiple_of(640 * zz, 128), 640)
        return b["n2"][:, :ROWS, cols].reshape(2 * ROWS, 640)

    def query_terms(zz):
        rows = rows_of(zz)
        for h in range(2):
            deltas = qd[:, :, :, 256 * h : 256 * h + 256].reshape(2 * ROWS, 256)
            term = lax.dot_general(rows, deltas, across, preferred_element_type=F32)
            b["gq"][h, zz] = term.astype(BF16).reshape(4, 160, 256)

    def key_terms(zz):
        rows = rows_of(zz)
        for h in range(2):
            deltas = jnp.concatenate(
                [
                    kvd[:, :, :, 128 * h : 128 * h + 128],
                    kvd[:, :, :, 256 + 128 * h : 384 + 128 * h],
                ],
                axis=-1,
            ).reshape(2 * ROWS, 256)
            term = lax.dot_general(rows, deltas, across, preferred_element_type=F32)
            term = term.astype(BF16).reshape(4, 2, 80, 256)
            for i in range(2):
                b["gkv"][i, h, zz] = term[:, i]

    def owners(end, rows, at_y):
        sends = []
        for h in range(2):
            for i in range(2):
                goal = 2 * j + h
                here = jnp.logical_and(goal == (y if at_y else z), i == j)
                device = dev(goal, z, x, i) if at_y else dev(y, goal, x, i)
                sends.append((end.at[h, pl.ds(rows * i, rows)], y if at_y else z, device, here))
        return sends

    def rest(w_buf, tok, cot, acc):
        def get_weights(first):
            return [
                get(w_h.at[pl.ds(first, 4)], w_buf.at[0], 8),
                get(wother_h.at[pl.ds(first, 4)], w_buf.at[1], 9),
            ]

        side = get_weights(0) + [get(tok_h, tok, 10), get(cot_h, cot, 11)]
        for cp in side:
            cp.start()

        def tiles(first, last, mine, other, fresh):
            @pl.loop(first, last)
            def _(n):
                total = None
                for half, lhs in enumerate((mine, other)):
                    rhs = jnp.concatenate(
                        [w_buf[half, m, rows_at(512 * n, 512), :] for m in range(4)], axis=-1
                    )
                    term = lax.dot_general(lhs, rhs, apart, preferred_element_type=F32)
                    total = term if total is None else total + term
                acc[n] = total if fresh else acc[n] + total

        def norm_rows(part):
            @pl.loop(12 * part, 12 * part + 12)
            def _(k):
                at = rows_at(k * 16, 16)
                t = tok[at, :].astype(F32)
                grad = jnp.concatenate([acc[m, at, :] for m in range(5)], axis=-1)
                h = grad * gain[...]
                scale = lax.rsqrt(jnp.mean(t * t, axis=-1, keepdims=True) + EPS)
                middle = jnp.mean(h * t, axis=-1, keepdims=True)
                turned = scale * h - t * (scale * scale * scale * middle)
                cot[at, :] = (cot[at, :].astype(F32) + turned).astype(BF16)

            at = pl.ds(192 * part, 192)
            cp = pltpu.make_async_copy(cot.at[at], out_h.at[at], b["put"].at[part])
            cp.start()
            return cp

        relay_step(0)
        get(n2_h, b["n2"], 6).wait()
        query_terms(up(z, 2))
        q1.start()
        relay_step(1)
        query_terms(up(z, 1))
        query_terms(up(z, 3))
        relay_step(2)
        query_terms(z)
        for cp in side[:2]:
            cp.wait()
        for s in range(3):
            give_delta(0, s).wait_recv()
        tiles(0, 5, qd[j].reshape(ROWS, 512), b["dq"][...].reshape(ROWS, 512), True)
        later = get_weights(4)
        for cp in later:
            cp.start()
        q1.forward()
        b["o_mid"][...] = o1.finish().astype(BF16)
        o2.start()
        near_step(0)
        near_step(1)
        near_step(2)
        o2.forward()
        get(raw_h.at[2], b["raw_k"], 7).wait()
        total_step(0)
        total_step(1)
        b["q_mid"][...] = q1.finish().astype(BF16)
        q2.start()
        total_step(2)
        key_terms(up(z, 2))
        k1[0].start()
        key_terms(up(z, 1))
        key_terms(up(z, 3))
        q2.forward()
        key_terms(z)
        k1[1].start()
        b["o_end"][...] = o2.finish().astype(BF16)
        o_sends = owners(b["o_end"], 32, False)
        send_last(b["o_end"], b["o_land"], o_sends, b["ls"].at[0], b["lr"].at[0], b["lc"].at[0], True)
        k1[0].forward()
        for cp in later:
            cp.wait()
        for s in range(3):
            give_delta(1, s).wait_recv()
        kv_mine, kv_other = kvd[j].reshape(ROWS, 512), b["dkv"][...].reshape(ROWS, 512)
        tiles(0, 3, kv_mine, kv_other, False)
        k1[1].forward()
        b["q_end"][...] = q2.finish().astype(BF16)
        q_sends = owners(b["q_end"], 80, True)
        send_last(b["q_end"], b["q_land"], q_sends, b["ls"].at[1], b["lr"].at[1], b["lc"].at[1], True)
        tiles(3, 5, kv_mine, kv_other, False)
        for cp in side[2:]:
            cp.wait()
        b["k_mid"][0] = k1[0].finish().astype(BF16)
        k2[0].start()
        puts = [norm_rows(0)]
        b["k_mid"][1] = k1[1].finish().astype(BF16)
        k2[1].start()
        k2[0].forward()
        puts.append(norm_rows(1))
        k2[1].forward()
        k_sends = []
        for f in range(2):
            b["k_end"][f] = k2[f].finish().astype(BF16)
            for h in range(2):
                goal = 2 * j + h
                here = jnp.logical_and(goal == y, f == j)
                k_sends.append((b["k_end"].at[f, h], y, dev(goal, z, x, f), here))
        send_last(b["k_end"], b["k_land"], k_sends, b["ls"].at[2], b["lr"].at[2], b["lc"].at[2], True)
        flows = (
            (o_sends, b["o_end"].at[0, pl.ds(0, 32)], b["o_end"], b["o_land"], z, oo),
            (q_sends, b["q_end"].at[0, pl.ds(0, 80)], b["q_end"], b["q_land"], y, oq),
            (k_sends, b["k_end"].at[0, 0], b["k_end"], b["k_land"], y, okv),
        )
        for n, (sends, like, end, land, me, out) in enumerate(flows):
            ls, lr, lc = b["ls"].at[n], b["lr"].at[n], b["lc"].at[n]
            send_last(end, land, sends, ls, lr, lc, False)
            sum_last(like, land, ls, lr, me, lax.div(me, 2) == j, partner, out)
        for cp in puts:
            cp.wait()

    pl.run_scoped(
        rest,
        pltpu.VMEM((2, 4, D, 128), BF16),
        pltpu.VMEM((ROWS, D), BF16),
        pltpu.VMEM((ROWS, D), BF16),
        pltpu.VMEM((5, ROWS, 512), F32),
    )
    for s in range(3):
        for i in range(2):

            @pl.when(low)
            def _():
                relay_right(i, s).wait_send()

            @pl.when(jnp.logical_not(low))
            def _():
                relay_left(i, s).wait_send()

            to_left(i, s).wait_send()
            to_right(i, s).wait_send()
            back(i, s).wait_send()
        for f in range(2):
            give_delta(f, s).wait_send()
    for ring in [o1, o2, q1, q2] + k1 + k2:
        ring.drain()


def tail(q, unit, halo, soft, grad, raw, cos, sin, gains, go, n2, w, wother, tok, cot, gain):
    return comm_call(
        tail_kernel,
        "tail",
        2,
        (sds((32, 640), F32), sds((80, 256), F32), sds((80, 256), F32), sds((ROWS, D), BF16)),
        [pltpu.VMEM(*spec) for spec in TAIL.values()] + [DMA(n) for n in TAIL_SEMS.values()],
        "hhhhhhvvvhhhhhhv",
        "vvvh",
    )(
        q.reshape(2, 2, 3, 128, 256),
        unit,
        halo,
        soft,
        grad,
        raw.reshape(3, 2, 3, 128, 256),
        cos.reshape(2, 3, 128, 128),
        sin.reshape(2, 3, 128, 128),
        gains,
        go,
        n2,
        w,
        wother,
        tok,
        cot,
        gain,
    )


def per_device(
    tokens,
    doc_ids,
    cotangent,
    input_gain,
    query_weight,
    key_weight,
    value_weight,
    output_weight,
    query_gain,
    key_gain,
    post_gain,
):
    seq_count, shard_size, width = tokens.shape
    c = lax.axis_index("ctx")
    core = lax.rem(c, 2)
    tok = tokens.reshape(ROWS, D)
    cot = cotangent.reshape(ROWS, D)
    wide = tok.astype(F32)
    scale = lax.rsqrt(jnp.mean(wide * wide, axis=-1, keepdims=True) + EPS)
    normed = (wide * scale * input_gain).astype(BF16)
    line = jnp.pad(doc_ids.reshape(1, ROWS).astype(BF16), ((0, 0), (0, D - ROWS)))
    at = lax.broadcasted_iota(jnp.int32, (NOTE_ROWS, 1), 0)
    notes = jnp.where(at == 8 * core, line, jnp.zeros((), BF16))
    noted = jnp.concatenate([normed, notes], axis=0)

    start = lax.div(c, 2) * 256
    positions = (start + jnp.arange(256, dtype=jnp.int32)).astype(F32)
    exponents = jnp.arange(128, dtype=jnp.int32).astype(F32) * (2.0 / 256)
    angles = positions[:, None] * ROPE_BASE ** (-exponents)

    def table(values):
        values = values.reshape(2, 1, 128, 128)
        return jnp.broadcast_to(values, (2, 3, 128, 128)).reshape(2 * ROWS, 128)

    cos, sin = table(jnp.cos(angles)), table(jnp.sin(angles))
    gains = jnp.pad(jnp.stack([query_gain, key_gain]), ((0, 6), (0, 0)))
    base = jnp.full((8, 128), start, jnp.int32)

    n2, w = gather(noted, query_weight, key_weight, value_weight)
    q, unit, raw = project(n2, w, cos, sin, gains)
    halo, wo, wother = exchange_halo(unit, output_weight.reshape(2, 128, D), w)
    layer_out, grad, go, soft = middle(
        q, unit, halo, base, wo.reshape(1024, D), tok, cot, post_gain.reshape(1, D)
    )
    oo, oq, okv, tokens_grad = tail(
        q, unit, halo, soft, grad, raw, cos, sin, gains, go, n2, w, wother, tok, cot,
        input_gain.reshape(1, D),
    )
    shape = (seq_count, shard_size, width)
    return (
        layer_out.reshape(shape),
        tokens_grad.reshape(shape),
        oq,
        okv[:, :128],
        okv[:, 128:],
        oo,
    )


def solution(mesh):
    placed = (
        P("fsdp", "ctx", None),
        P("fsdp", "ctx"),
        P("fsdp", "ctx", None),
        P(),
        P("fsdp", None),
        P("fsdp", None),
        P("fsdp", None),
        P("fsdp", None),
        P(),
        P(),
        P(),
    )
    return jax.shard_map(
        per_device,
        mesh=mesh,
        in_specs=placed,
        out_specs=(
            P("fsdp", "ctx", None),
            P("fsdp", "ctx", None),
            P("ctx", "fsdp"),
            P("ctx", "fsdp"),
            P("ctx", "fsdp"),
            P("ctx", "fsdp"),
        ),
        check_vma=False,
    )
```
